512 devices in a mesh: atoms: 128 (over x_hi, z, y), modes: 4 (over x_lo, core).
Axes of the slice: x: 4 (x_hi: 2, x_lo: 2; x = x_hi * 2 + x_lo), y: 8, z: 8, core: 2. Of those that a mesh axis runs over, the one named last changes fastest.
Arguments:
- eigvec: bfloat16 [49152, 2048], P('atoms', 'modes'), may hold values from -6 to 6
- operator_blocks: bfloat16 [384, 8, 128, 128], P('atoms'), may hold values from -0.0008544922 to 0.0008544922
- column_blocks: int32 [384, 8], P('atoms'), may hold values from 0 to 383, as said below
- block_mask: int32 [384, 8], P('atoms'), may hold values 0 or 1
- spectrum: float32 [49152], replicated, may hold values from 0.5 to 20
- mode_index: int32 [2048], replicated, may hold values from 0 to 49151
- linewidth: float32 [2048], replicated, may hold values from 0.05 to 1
Outputs:
- flux_tiles: float32 [2048, 2048], P('modes', 'atoms')
- diffusivity: float32 [2048], P('modes')
The draws below stay inside these ranges and needn't reach their ends.
Inputs may be any that keep to these rules, and one draw needn't show every extreme that they name: `column_blocks`: the 8 column blocks of row block r are distinct and lie within 4 blocks of r, counted around the cycle of 384 blocks.
All inputs are finite; a program needn't handle non-finite values. No bound on the sum of `block_mask` on one device may be relied on, other than what follows from the above.
Results may differ from the reference program's by a relative error of at most 0.0058.
Values may be sent and summed in bfloat16 or wider, within the bound.
A program may use at most 64 MiB of HBM per device.

```python
import math
import jax
import jax.numpy as jnp
from jax import lax

BS = 128
SLOTS = 8
REACH = 4
M = 2048
NB = 384
COORDS = 49152


def draw_column_blocks(key, part):
    candidates = 2 * REACH + 1
    random_bits = jax.random.randint(key, (NB, candidates), 0, 2 ** 20)
    scores = random_bits * candidates + jnp.arange(candidates, dtype=jnp.int32)[None, :]
    chosen = jnp.argsort(scores, axis=1)[:, :SLOTS].astype(jnp.int32)
    row_blocks = jnp.arange(NB, dtype=jnp.int32)[:, None]
    return ((row_blocks + chosen - REACH) % NB).astype(jnp.int32)


def touch_ends(array, stream_key, smallest, largest):
    spot = [jax.random.randint(jax.random.fold_in(stream_key, axis), (), 0, length) for axis, length in enumerate(array.shape)]
    widest = array.shape.index(max(array.shape))
    next_to = spot[:widest] + [(spot[widest] + 1) % array.shape[widest]] + spot[widest + 1:]
    return array.at[tuple(spot)].set(smallest).at[tuple(next_to)].set(largest)


def shard_levels(own_key, shape, shards, least, high):
    factor_of, own = 1.0, jax.random.fold_in(own_key, 6)
    for axis_at, shards_of in shards:
        steps = jnp.exp(jax.random.uniform(jax.random.fold_in(own, axis_at), (shards_of,), jnp.float32, least / len(shards), high / len(shards)))
        factor_of = factor_of * jnp.repeat(steps, shape[axis_at] // shards_of).reshape([-1 if axis == axis_at else 1 for axis in range(len(shape))])
    return factor_of


def noise(rng, shape, width, most, shards=(), kind=jnp.bfloat16):
    values = width * jax.random.normal(rng, shape, jnp.float32)
    if shards:
        values = values * shard_levels(rng, shape, shards, -0.22, 0.18)
    return jnp.clip(values, -most, most).astype(kind)


def setup_inputs(seed: int = 0) -> dict:
    splits = jax.random.split(jax.random.key(seed), 8)
    eigvec = noise(splits[0], (COORDS, M), 1.0, 6.0, ((0, 128), (1, 4)))
    operator_blocks = noise(splits[1], (NB, SLOTS, BS, BS), (SLOTS * BS * COORDS) ** -0.5, 0.0008544922, ((0, 128),))
    column_blocks = draw_column_blocks(jax.random.fold_in(splits[7], 71), 0)
    block_mask = touch_ends((jax.random.randint(splits[3], (NB, SLOTS), 0, 4) < 3).astype(jnp.int32), jax.random.fold_in(splits[3], 1), 0, 1)
    spectrum = jnp.clip(jnp.exp(jax.random.uniform(splits[4], (COORDS,), jnp.float32, math.log(0.5), math.log(20.0))), 0.5, 20.0)
    mode_index = touch_ends(jax.random.randint(splits[5], (M,), 0, COORDS), jax.random.fold_in(splits[5], 1), 0, COORDS - 1).astype(jnp.int32)
    linewidth = jnp.clip(jnp.exp(jax.random.uniform(splits[6], (M,), jnp.float32, math.log(0.05), math.log(1.0))), 0.05, 1.0)
    return dict(eigvec=eigvec, operator_blocks=operator_blocks, column_blocks=column_blocks, block_mask=block_mask, spectrum=spectrum, mode_index=mode_index, linewidth=linewidth)


def pair_weight(row_freq, col_freq, row_width, col_width):
    freq_sum = row_freq[:, None] + col_freq[None, :]
    spacing = row_freq[:, None] - col_freq[None, :]
    mean_width = 0.5 * (row_width[:, None] + col_width[None, :])
    factor = freq_sum * freq_sum / (4.0 * row_freq[:, None] * col_freq[None, :])
    return factor * mean_width / (spacing * spacing + mean_width * mean_width)


def reference(eigvec, operator_blocks, column_blocks, block_mask, spectrum, mode_index, linewidth):
    eig_blocks = eigvec.reshape(NB, BS, M)
    masked = jnp.where(block_mask[:, :, None, None] > 0, operator_blocks, jnp.zeros((), operator_blocks.dtype))
    product = jnp.zeros((NB, BS, M), jnp.float32)
    for slot_index in range(SLOTS):
        picked = eig_blocks[column_blocks[:, slot_index]]
        product = product + jnp.einsum("bij,bjm->bim", masked[:, slot_index].astype(jnp.float32), picked.astype(jnp.float32), precision=lax.Precision.HIGHEST)
    velocity = product.reshape(COORDS, M).astype(jnp.bfloat16)
    eig_float = eigvec.astype(jnp.float32)
    vel_float = velocity.astype(jnp.float32)
    pair_sum = jnp.dot(eig_float.T, vel_float, precision=lax.Precision.HIGHEST)
    flux_tiles = pair_sum - pair_sum.T
    frequency = spectrum[mode_index]
    weight = pair_weight(frequency, frequency, linewidth, linewidth)
    diffusivity = jnp.sum(weight * flux_tiles * flux_tiles, axis=1) / M
    return flux_tiles, diffusivity
```

```python
import functools

import jax
import jax.numpy as jnp
from jax import lax
from jax.experimental import pallas as pl
from jax.experimental.pallas import tpu as pltpu
from jax.sharding import PartitionSpec as P

BF = jnp.bfloat16
F32 = jnp.float32
NX, NZ, NY = 2, 8, 8
ATOMS = NX * NZ * NY
REACH = 4
BAND = 2 * REACH + 1
BS = 128
LB = 3
UP = ((0, 7), (0, 8), (1, 6), (1, 7), (1, 8), (2, 5), (2, 6), (2, 7), (2, 8))
DOWN = ((0, 1), (0, 2), (0, 3), (1, 0), (1, 1), (1, 2), (2, 0), (2, 1), (0, 0))


def kernel(
    e_hbm, op_hbm, col_s, mask_s, spec_ref, midx_ref, width_ref,
    tile_ref, diff_ref,
    ext, others, turned, opv, dense, up_send, dn_send, lo_blk, hi_blk, lo_far, hi_far,
    bmat, wmat, pz, py, rz_plus, rz_minus, ry_plus, ry_minus, z_mid, y_mid, z_in, y_in,
    s_y, s_xz,
    load_sem, halo_send, halo_recv, mode_send, mode_recv, blk_send, blk_recv,
    ring_send, ring_recv, far_send, far_recv, sum_send, sum_recv,
):
    me = lax.axis_index("atoms")
    mode = lax.axis_index("modes")
    x_lo, core = mode // 2, mode % 2
    x, z, y = me // (NZ * NY), (me // NY) % NZ, me % NY
    above = ((me + 1) % ATOMS, mode)
    below = ((me + ATOMS - 1) % ATOMS, mode)
    twin = (me, x_lo * 2 + 1 - core)
    across = (me, (1 - x_lo) * 2 + core)
    twin_mode = x_lo * 2 + 1 - core
    across_mode = (1 - x_lo) * 2 + core
    last_mode = (1 - x_lo) * 2 + 1 - core

    def at_y(o):
        return (x * (NZ * NY) + z * NY + (y + o) % NY, mode)

    def at_z(o):
        return (x * (NZ * NY) + ((z + o) % NZ) * NY + y, mode)

    gz = x * NZ + z
    gy = x * NY + y

    def group_xz(o):
        g = (gz + o) % 16
        return g, (g * NY + y, mode)

    def group_xy(o):
        g = (gy + o) % 16
        return g, ((g // NY) * (NZ * NY) + z * NY + g % NY, mode)

    def remote(src, dst, ssem, rsem, device):
        return pltpu.make_async_remote_copy(
            src_ref=src, dst_ref=dst, send_sem=ssem, recv_sem=rsem,
            device_id=device, device_id_type=pl.DeviceIdType.MESH,
        )

    barrier = pltpu.get_barrier_semaphore()

    def greet(device):
        pl.semaphore_signal(
            barrier, inc=1, device_id=device, device_id_type=pl.DeviceIdType.MESH
        )

    for device in (above, below, twin, across):
        greet(device)

    def greet_far(o, carry):
        greet(group_xz(o)[1])
        greet(group_xy(o)[1])
        return carry

    lax.fori_loop(1, 16, greet_far, 0)

    load_op = pltpu.make_async_copy(op_hbm, opv, load_sem.at[0])
    load_op.start()
    load_e = [
        pltpu.make_async_copy(e_hbm.at[pl.ds(b * BS, BS)], ext.at[REACH + b], load_sem.at[1 + b])
        for b in range(LB)
    ]
    for copy in load_e:
        copy.start()

    load_op.wait()
    for r in range(LB):
        for d in range(BAND):
            target = (me * LB + r + d - REACH + ATOMS * LB) % (ATOMS * LB)
            slot = jnp.int32(0)
            used = jnp.int32(0)
            for s in range(8):
                hit = col_s[r, s] == target
                slot = jnp.where(hit, s, slot)
                used = jnp.where(hit, mask_s[r, s], used)
            keep = jnp.where(used > 0, F32(1), F32(0)).astype(F32)
            block = (opv[r, slot].astype(F32) * keep).astype(BF)
            dense[r, d] = block
            if (r, d) in UP:
                up_send[UP.index((r, d))] = block
            if (r, d) in DOWN:
                dn_send[DOWN.index((r, d))] = block
    up_send[9] = jnp.zeros((BS, BS), BF)
    dn_send[9] = jnp.zeros((BS, BS), BF)

    pl.semaphore_wait(barrier, 34)

    sends = []

    def go(*args):
        copy = remote(*args)
        copy.start()
        sends.append(copy)
        return copy

    go(e_hbm, others.at[0], mode_send.at[0], mode_recv.at[0], across)
    go(e_hbm, others.at[1], mode_send.at[1], mode_recv.at[1], twin)
    half = pl.ds(core * 5, 5)
    go(up_send.at[half], lo_blk.at[half], blk_send.at[0], blk_recv.at[0], above)
    go(dn_send.at[half], hi_blk.at[half], blk_send.at[1], blk_recv.at[1], below)
    for b in (2, 1, 0):
        go(e_hbm.at[pl.ds(b * BS, BS)], ext.at[1 + b], halo_send.at[b], halo_recv.at[b], above)
        t = 2 - b
        go(e_hbm.at[pl.ds(t * BS, BS)], ext.at[7 + t], halo_send.at[3 + t], halo_recv.at[3 + t], below)

    def arrived(dst, sem):
        remote(dst, dst, sem, sem, above).wait_recv()

    arrived(ext.at[3], halo_recv.at[2])
    go(ext.at[3], ext.at[0], halo_send.at[6], halo_recv.at[6], above)
    arrived(ext.at[7], halo_recv.at[3])
    go(ext.at[7], ext.at[10], halo_send.at[7], halo_recv.at[7], below)

    arrived(lo_blk.at[half], blk_recv.at[0])
    go(lo_blk.at[half], lo_blk.at[half], blk_send.at[2], blk_recv.at[2], twin)
    arrived(hi_blk.at[half], blk_recv.at[1])
    go(hi_blk.at[half], hi_blk.at[half], blk_send.at[3], blk_recv.at[3], twin)
    other_half = pl.ds((1 - core) * 5, 5)
    arrived(lo_blk.at[other_half], blk_recv.at[2])
    go(lo_blk.at[8], lo_far, blk_send.at[4], blk_recv.at[4], above)
    arrived(hi_blk.at[other_half], blk_recv.at[3])
    go(hi_blk.at[8], hi_far, blk_send.at[5], blk_recv.at[5], below)

    def build(r, d, mirror):
        value = mirror.astype(F32).T - dense[r, d].astype(F32)
        bmat[r, :, d * BS : (d + 1) * BS] = value.astype(BF)

    for r in range(LB):
        for c in range(LB):
            d = c - r + REACH
            build(r, d, dense[c, 2 * REACH - d])
    for k in range(8):
        c, d = UP[k]
        r = d + c - 7
        build(r, c + 1 - r, lo_blk[k])
        c, d = DOWN[k]
        r = d + c - 1
        build(r, c + 7 - r, hi_blk[k])

    def turn(slot_mode, get):
        for b in range(LB):
            turned[slot_mode, :, b * BS : (b + 1) * BS] = get(b).T

    for copy in load_e:
        copy.wait()
    turn(mode, lambda b: ext[REACH + b])
    arrived(others.at[1], mode_recv.at[1])
    turn(twin_mode, lambda b: others[1, b * BS : (b + 1) * BS, :])
    arrived(others.at[0], mode_recv.at[0])
    go(others.at[0], others.at[2], mode_send.at[2], mode_recv.at[2], twin)
    turn(across_mode, lambda b: others[0, b * BS : (b + 1) * BS, :])
    arrived(others.at[2], mode_recv.at[2])
    turn(last_mode, lambda b: others[2, b * BS : (b + 1) * BS, :])

    arrived(lo_far, blk_recv.at[4])
    build(0, 0, lo_far[...])
    arrived(hi_far, blk_recv.at[5])
    build(2, 8, hi_far[...])
    for index, sem in ((1, 0), (2, 1), (8, 4), (9, 5), (0, 6), (10, 7)):
        arrived(ext.at[index], halo_recv.at[sem])

    for r in range(LB):
        rows = ext[r : r + BAND].reshape(BAND * BS, 512)
        wmat[r * BS : (r + 1) * BS, :] = jnp.dot(
            bmat[r], rows, preferred_element_type=F32
        ).astype(BF)

    def product(mb, carry):
        part = jnp.dot(turned[mb], wmat[...], preferred_element_type=F32).astype(BF)
        for q in range(4):
            rows = part[q * BS : (q + 1) * BS]
            pz[(mb % 2) * 4 + q, pl.ds((mb // 2) * NY, NY)] = rows[:, :256].reshape(NY, 16, 256)
            py[:, mb * 4 + q] = rows[:, 256:].reshape(NY, 16, 256)
        return carry

    lax.fori_loop(0, 4, product, 0)

    A, B = 0, 1

    def index(sense, h, k):
        long = (h == A) if sense == 0 else (h == B)
        return 4 - k if long else 7 - k

    rings = (
        (pz, (rz_plus, rz_minus), z, (at_z(1), at_z(NZ - 1)), 0),
        (py, (ry_plus, ry_minus), y, (at_y(1), at_y(NY - 1)), 1),
    )

    def hand(ring, sense, h, k, src):
        _, recv, _, devices, r = ring
        i = index(sense, h, k)
        go(src, recv[sense].at[i], ring_send.at[r, sense, i], ring_recv.at[r, sense, i], devices[sense])

    def owner(ring, sense, k):
        return (ring[2] + (k if sense == 0 else 8 - k)) % 8

    for sense, h, k in ((0, A, 4), (1, B, 4), (0, B, 3), (1, A, 3)):
        for ring in rings:
            hand(ring, sense, h, k, ring[0].at[owner(ring, sense, k), pl.ds(h * 8, 8)])

    def take(ring, sense, h, k):
        i = index(sense, h, k)
        arrived(ring[1][sense].at[i], ring_recv.at[ring[4], sense, i])
        return i

    for k in (4, 3, 2):
        for sense, h, kk in ((0, A, k), (1, B, k), (0, B, k - 1), (1, A, k - 1)):
            if kk < 2:
                continue
            for ring in rings:
                i = take(ring, sense, h, kk)
                buf = ring[1][sense]
                mine = ring[0][owner(ring, sense, kk - 1), h * 8 : h * 8 + 8]
                buf[i] = (buf[i].astype(F32) + mine.astype(F32)).astype(BF)
                hand(ring, sense, h, kk - 1, buf.at[i])
    for h in (A, B):
        for ring, mid in zip(rings, (z_mid, y_mid)):
            i = take(ring, 0, h, 1)
            j = take(ring, 1, h, 1)
            mine = ring[0][ring[2], h * 8 : h * 8 + 8]
            mid[h * 8 : h * 8 + 8] = (
                mine.astype(F32) + ring[1][0][i].astype(F32) + ring[1][1][j].astype(F32)
            ).astype(BF)

    def direct_z(o):
        g, device = group_xy(o)
        return remote(z_mid.at[g], z_in.at[gy], far_send.at[0, g], far_recv.at[0, gy], device)

    def direct_y(o):
        g, device = group_xz(o)
        return remote(y_mid.at[g], y_in.at[gz], far_send.at[1, g], far_recv.at[1, gz], device)

    def send_direct(o, carry):
        direct_z(o).start()
        direct_y(o).start()
        return carry

    lax.fori_loop(1, 16, send_direct, 0)
    z_in[gy] = z_mid[gy]
    y_in[gz] = y_mid[gz]

    spot = lax.broadcasted_iota(jnp.int32, (16, 512), 0) + (me % 32) * 16
    on_tile = lax.broadcasted_iota(jnp.int32, (16, 512), 1) == spot

    def column(row):
        spread = jnp.where(on_tile, jnp.broadcast_to(row, (16, 512)), F32(0))
        return jnp.sum(spread, axis=1, keepdims=True)

    def frequency(block):
        at = midx_ref[block]
        high = lax.broadcasted_iota(jnp.int32, (384, 512), 0) == jnp.broadcast_to(at // 128, (384, 512))
        rows = lax.dot_general(
            spec_ref[...], high.astype(F32), (((0,), (0,)), ((), ())),
            precision=lax.Precision.HIGHEST, preferred_element_type=F32,
        )
        low = lax.broadcasted_iota(jnp.int32, (128, 512), 0) == jnp.broadcast_to(at % 128, (128, 512))
        return jnp.sum(jnp.where(low, rows, F32(0)), axis=0, keepdims=True)

    row_freq = frequency(mode)
    row_width = width_ref[mode]
    col_freq = column(frequency(me // 32))
    col_width = column(width_ref[me // 32])
    freq_sum = row_freq + col_freq
    spacing = row_freq - col_freq
    mean_width = 0.5 * (row_width + col_width)
    factor = freq_sum * freq_sum / (4.0 * row_freq * col_freq)
    weight = factor * mean_width / (spacing * spacing + mean_width * mean_width)

    def wait_direct(o, carry):
        g = (gy + o) % 16
        arrived(z_in.at[g], far_recv.at[0, g])
        g = (gz + o) % 16
        arrived(y_in.at[g], far_recv.at[1, g])
        return carry

    lax.fori_loop(1, 16, wait_direct, 0)
    tile = jnp.concatenate(
        [jnp.sum(z_in[...].astype(F32), axis=0), jnp.sum(y_in[...].astype(F32), axis=0)], axis=1
    )
    tile_ref[...] = tile
    share = jnp.sum(weight * tile * tile, axis=0, keepdims=True)

    def packed(slot):
        for q in range(4):
            slot[q : q + 1, :] = share[:, q * BS : (q + 1) * BS]
        slot[4:8, :] = jnp.zeros((4, BS), F32)

    packed(s_y.at[y])
    for o in range(1, NY):
        go(s_y.at[y], s_y.at[y], sum_send.at[o], sum_recv.at[y], at_y(o))

    def wait_y(o, carry):
        g = (y + o) % NY
        arrived(s_y.at[g], sum_recv.at[g])
        return carry

    lax.fori_loop(1, NY, wait_y, 0)
    s_xz[gz] = jnp.sum(s_y[...], axis=0)

    def sum_xz(o):
        return remote(
            s_xz.at[gz], s_xz.at[gz], sum_send.at[8 + o], sum_recv.at[8 + gz], group_xz(o)[1]
        )

    def send_xz(o, carry):
        sum_xz(o).start()
        return carry

    lax.fori_loop(1, 16, send_xz, 0)

    def wait_xz(o, carry):
        g = (gz + o) % 16
        arrived(s_xz.at[g], sum_recv.at[8 + g])
        return carry

    lax.fori_loop(1, 16, wait_xz, 0)
    diff_ref[...] = jnp.sum(s_xz[...], axis=0) * F32(1.0 / 2048)

    for copy in sends:
        copy.wait_send()

    def finish(o, carry):
        direct_z(o).wait_send()
        direct_y(o).wait_send()
        sum_xz(o).wait_send()
        return carry

    lax.fori_loop(1, 16, finish, 0)


def body(eigvec, operator_blocks, column_blocks, block_mask, spectrum, mode_index, linewidth):
    anywhere = pl.BlockSpec(memory_space=pl.ANY)
    scalars = pl.BlockSpec(memory_space=pltpu.SMEM)
    vmem = pl.BlockSpec(memory_space=pltpu.VMEM)
    dma = pltpu.SemaphoreType.DMA
    ring_buffer = pltpu.VMEM((7, 8, 16, 256), BF)
    tile, diff = pl.pallas_call(
        kernel,
        out_shape=(
            jax.ShapeDtypeStruct((16, 512), F32),
            jax.ShapeDtypeStruct((8, BS), F32),
        ),
        in_specs=[anywhere, anywhere, scalars, scalars, vmem, vmem, vmem],
        out_specs=(vmem, vmem),
        scratch_shapes=[
            pltpu.VMEM((11, BS, 512), BF),
            pltpu.VMEM((3, LB * BS, 512), BF),
            pltpu.VMEM((4, 512, LB * BS), BF),
            pltpu.VMEM((LB, 8, BS, BS), BF),
            pltpu.VMEM((LB, BAND, BS, BS), BF),
            pltpu.VMEM((10, BS, BS), BF),
            pltpu.VMEM((10, BS, BS), BF),
            pltpu.VMEM((10, BS, BS), BF),
            pltpu.VMEM((10, BS, BS), BF),
            pltpu.VMEM((BS, BS), BF),
            pltpu.VMEM((BS, BS), BF),
            pltpu.VMEM((LB, BS, BAND * BS), BF),
            pltpu.VMEM((LB * BS, 512), BF),
            pltpu.VMEM((NZ, 16, 16, 256), BF),
            pltpu.VMEM((NY, 16, 16, 256), BF),
            ring_buffer, ring_buffer, ring_buffer, ring_buffer,
            pltpu.VMEM((16, 16, 256), BF),
            pltpu.VMEM((16, 16, 256), BF),
            pltpu.VMEM((16, 16, 256), BF),
            pltpu.VMEM((16, 16, 256), BF),
            pltpu.VMEM((NY, 8, BS), F32),
            pltpu.VMEM((16, 8, BS), F32),
            dma((4,)), dma((8,)), dma((8,)), dma((3,)), dma((3,)), dma((6,)), dma((6,)),
            dma((2, 2, 7)), dma((2, 2, 7)), dma((2, 16)), dma((2, 16)), dma((24,)), dma((24,)),
        ],
        compiler_params=pltpu.CompilerParams(
            collective_id=0, has_side_effects=True, vmem_limit_bytes=40 * 1024 * 1024
        ),
    )(
        eigvec, operator_blocks, column_blocks, block_mask,
        spectrum.reshape(384, 128), mode_index.reshape(4, 1, 512), linewidth.reshape(4, 1, 512),
    )
    return tile.T, diff[:4].reshape(512)


def solution(mesh):
    in_specs = (
        P("atoms", "modes"),
        P("atoms", None, None, None),
        P("atoms", None),
        P("atoms", None),
        P(),
        P(),
        P(),
    )
    out_specs = (P("modes", "atoms"), P("modes"))
    return jax.shard_map(body, mesh=mesh, in_specs=in_specs, out_specs=out_specs, check_vma=False)
```

```python
import functools

import jax
import jax.numpy as jnp
from jax import lax
from jax.experimental import pallas as pl
from jax.experimental.pallas import tpu as pltpu
from jax.sharding import PartitionSpec as P

BF = jnp.bfloat16
F32 = jnp.float32
NX, NZ, NY = 2, 8, 8
ATOMS = NX * NZ * NY
REACH = 4
BAND = 2 * REACH + 1
BS = 128
LB = 3
UP = ((0, 7), (0, 8), (1, 6), (1, 7), (1, 8), (2, 5), (2, 6), (2, 7), (2, 8))
DOWN = ((0, 1), (0, 2), (0, 3), (1, 0), (1, 1), (1, 2), (2, 0), (2, 1), (0, 0))


def kernel(
    e_hbm, op_hbm, col_hbm, mask_hbm, spec_hbm, midx_hbm, width_hbm,
    tile_ref, diff_ref,
    ext, others, turned, opv, col_s, mask_s, spec_ref, midx_ref, width_ref,
    dense, up_send, dn_send, lo_blk, hi_blk, lo_far, hi_far,
    bmat, wmat, pz, py, rz_plus, rz_minus, ry_plus, ry_minus, z_mid, y_mid, z_in, y_in,
    s_y, s_xz,
    load_sem, mode_send, mode_recv, blk_send, blk_recv, msg_send, msg_recv,
    ring_send, ring_recv, far_send, far_recv, sum_send, sum_recv,
):
    me = lax.axis_index("atoms")
    mode = lax.axis_index("modes")
    x_lo, core = mode // 2, mode % 2
    x, z, y = me // (NZ * NY), (me // NY) % NZ, me % NY
    above = ((me + 1) % ATOMS, mode)
    below = ((me + ATOMS - 1) % ATOMS, mode)
    twin = (me, x_lo * 2 + 1 - core)
    across = (me, (1 - x_lo) * 2 + core)
    twin_mode = x_lo * 2 + 1 - core
    across_mode = (1 - x_lo) * 2 + core
    last_mode = (1 - x_lo) * 2 + 1 - core

    def at_y(o):
        return (x * (NZ * NY) + z * NY + (y + o) % NY, mode)

    def at_z(o):
        return (x * (NZ * NY) + ((z + o) % NZ) * NY + y, mode)

    gz = x * NZ + z
    gy = x * NY + y

    def group_xz(o):
        g = (gz + o) % 16
        return g, (g * NY + y, mode)

    def group_xy(o):
        g = (gy + o) % 16
        return g, ((g // NY) * (NZ * NY) + z * NY + g % NY, mode)

    top = (y == NY - 1) & (z == NZ - 1)
    bottom = (y == 0) & (z == 0)
    above_across = ((me + 1) % ATOMS, across_mode)
    below_across = ((me + ATOMS - 1) % ATOMS, across_mode)

    def remote(src, dst, ssem, rsem, device):
        return pltpu.make_async_remote_copy(
            src_ref=src, dst_ref=dst, send_sem=ssem, recv_sem=rsem,
            device_id=device, device_id_type=pl.DeviceIdType.MESH,
        )

    loads = (
        (op_hbm, opv), (col_hbm, col_s), (mask_hbm, mask_s),
        (e_hbm.at[:, pl.ds(0, 256)], ext.at[0, pl.ds(REACH * BS, LB * BS)]),
        (e_hbm.at[:, pl.ds(256, 256)], ext.at[1, pl.ds(REACH * BS, LB * BS)]),
        (spec_hbm, spec_ref), (midx_hbm, midx_ref), (width_hbm, width_ref),
    )
    loads = [pltpu.make_async_copy(a, b, load_sem.at[i]) for i, (a, b) in enumerate(loads)]
    for copy in loads:
        copy.start()

    barrier = pltpu.get_barrier_semaphore()

    def greet(device):
        pl.semaphore_signal(
            barrier, inc=1, device_id=device, device_id_type=pl.DeviceIdType.MESH
        )

    for device in (above, below, twin, across):
        greet(device)
    greet(((me + 2) % ATOMS, mode))
    greet(((me + ATOMS - 2) % ATOMS, mode))
    for o in range(1, 16):
        greet(group_xz(o)[1])
        greet(group_xy(o)[1])

    @pl.when(top)
    def _():
        greet(above_across)

    @pl.when(bottom)
    def _():
        greet(below_across)

    extra = jnp.where(top | bottom, 1, 0)

    for copy in loads[:3]:
        copy.wait()
    for r in range(LB):
        for d in range(BAND):
            target = (me * LB + r + d - REACH + ATOMS * LB) % (ATOMS * LB)
            slot = jnp.int32(0)
            used = jnp.int32(0)
            for s in range(8):
                hit = col_s[r, s] == target
                slot = jnp.where(hit, s, slot)
                used = jnp.where(hit, mask_s[r, s], used)
            keep = jnp.where(used > 0, F32(1), F32(0)).astype(F32)
            block = (opv[r, slot].astype(F32) * keep).astype(BF)
            dense[r, d] = block
            if (r, d) in UP:
                up_send[UP.index((r, d))] = block
            if (r, d) in DOWN:
                dn_send[DOWN.index((r, d))] = block
    up_send[9] = jnp.zeros((BS, BS), BF)
    dn_send[9] = jnp.zeros((BS, BS), BF)

    pl.semaphore_wait(barrier, 36 + extra)

    sends = []

    def go(*args):
        copy = remote(*args)
        copy.start()
        sends.append(copy)
        return copy

    def arrived(dst, sem):
        remote(dst, dst, sem, sem, above).wait_recv()

    half = pl.ds(core * 5, 5)
    other_half = pl.ds((1 - core) * 5, 5)
    messages = [[(up_send.at[half], lo_blk.at[half])], [(dn_send.at[half], hi_blk.at[half])]]
    for h in range(2):
        lanes = pl.ds(h * 256, 256)
        rows = ext.at[h]
        messages[0] += [
            (e_hbm.at[pl.ds(256, 128), lanes], rows.at[pl.ds(384, 128)]),
            (e_hbm.at[pl.ds(0, 256), lanes], rows.at[pl.ds(128, 256)]),
            (rows.at[pl.ds(384, 128)], rows.at[pl.ds(0, 128)]),
        ]
        messages[1] += [
            (e_hbm.at[pl.ds(0, 128), lanes], rows.at[pl.ds(896, 128)]),
            (e_hbm.at[pl.ds(128, 256), lanes], rows.at[pl.ds(1024, 256)]),
            (rows.at[pl.ds(896, 128)], rows.at[pl.ds(1280, 128)]),
        ]
        if h == 0:
            messages[0].append((up_send.at[8], lo_far))
            messages[1].append((dn_send.at[8], hi_far))

    def tell(way, i):
        src, dst = messages[way][i]
        atoms, edge = (above[0], top) if way == 0 else (below[0], bottom)
        to_mode = jnp.where(edge, across_mode, mode) if i == 0 else mode
        if i == 4:
            atoms = (me + (2 if way == 0 else ATOMS - 2)) % ATOMS
        copy = remote(src, dst, msg_send.at[way, i], msg_recv.at[way, i], (atoms, to_mode))
        sends.append(copy)
        if i in (1, 2, 5, 6):
            pl.when(jnp.logical_not(edge))(copy.start)
        else:
            copy.start()

    def tell_both(i):
        tell(0, i)
        tell(1, i)

    def tell_for_across(way, i):
        h = i // 4
        start, count = (((256, 128), (0, 256)) if way == 0 else ((0, 128), (128, 256)))[i % 4 - 1]
        src = others.at[0, pl.ds(start, count), pl.ds(h * 256, 256)]
        remote(
            src, messages[way][i][1], msg_send.at[way, i], msg_recv.at[way, i],
            (above_across, below_across)[way],
        ).start()

    def lanes_of(h):
        return others.at[0, :, pl.ds(h * 256, 256)]

    def gather_arrived(h):
        arrived(lanes_of(h), mode_recv.at[h])

    def relay(h):
        for way, edge in ((0, top), (1, bottom)):

            @pl.when(edge)
            def _():
                gather_arrived(h)
                tell_for_across(way, 4 * h + 1)
                tell_for_across(way, 4 * h + 2)

    def hear(way, i):
        arrived(messages[way][i][1], msg_recv.at[way, i])

    for h in range(2):
        go(e_hbm.at[:, pl.ds(h * 256, 256)], lanes_of(h), mode_send.at[h], mode_recv.at[h], across)
    go(e_hbm, others.at[1], mode_send.at[2], mode_recv.at[2], twin)
    for i in (0, 1, 2, 4, 5):
        tell_both(i)

    def turn(slot_mode, b, block):
        turned[slot_mode, :, b * BS : (b + 1) * BS] = block.T

    def build(r, d, mirror):
        value = mirror.astype(F32).T - dense[r, d].astype(F32)
        bmat[r, :, d * BS : (d + 1) * BS] = value.astype(BF)

    for copy in loads[3:]:
        copy.wait()
    for r in range(LB):
        for c in range(LB):
            d = c - r + REACH
            build(r, d, dense[c, 2 * REACH - d])
    for b in range(LB):
        for h in range(2):
            turned[mode, h * 256 : (h + 1) * 256, b * BS : (b + 1) * BS] = ext[
                h, (REACH + b) * BS : (REACH + b + 1) * BS
            ].T

    relay(0)
    hear(0, 0)
    go(lo_blk.at[half], lo_blk.at[half], blk_send.at[0], blk_recv.at[0], twin)
    hear(1, 0)
    go(hi_blk.at[half], hi_blk.at[half], blk_send.at[1], blk_recv.at[1], twin)
    hear(0, 1)
    tell(0, 3)
    hear(1, 1)
    tell(1, 3)
    tell_both(6)
    relay(1)

    arrived(lo_blk.at[other_half], blk_recv.at[0])
    arrived(hi_blk.at[other_half], blk_recv.at[1])
    for k in range(8):
        c, d = UP[k]
        r = d + c - 7
        build(r, c + 1 - r, lo_blk[k])
        c, d = DOWN[k]
        r = d + c - 1
        build(r, c + 7 - r, hi_blk[k])

    arrived(others.at[1], mode_recv.at[2])
    for b in range(LB):
        turn(twin_mode, b, others[1, b * BS : (b + 1) * BS, :])
    for h in range(2):
        pl.when(jnp.logical_not(top | bottom))(functools.partial(gather_arrived, h))
        half_lanes = pl.ds(h * 256, 256)
        go(lanes_of(h), others.at[2, :, half_lanes], mode_send.at[3 + h], mode_recv.at[3 + h], twin)
        for b in range(LB):
            turned[across_mode, h * 256 : (h + 1) * 256, b * BS : (b + 1) * BS] = others[
                0, b * BS : (b + 1) * BS, h * 256 : (h + 1) * 256
            ].T
    for h in range(2):
        arrived(others.at[2, :, pl.ds(h * 256, 256)], mode_recv.at[3 + h])
        for b in range(LB):
            turned[last_mode, h * 256 : (h + 1) * 256, b * BS : (b + 1) * BS] = others[
                2, b * BS : (b + 1) * BS, h * 256 : (h + 1) * 256
            ].T

    hear(0, 4)
    build(0, 0, lo_far[...])
    hear(1, 4)
    build(2, 8, hi_far[...])

    def apply_operator(h):
        for r in range(LB):
            wmat[h, r * BS : (r + 1) * BS, :] = jnp.dot(
                bmat[r], ext[h, r * BS : (r + BAND) * BS], preferred_element_type=F32
            ).astype(BF)

    def product(h):
        def step(mb, carry):
            part = jnp.dot(turned[mb], wmat[h], preferred_element_type=F32).astype(BF)
            for q in range(4):
                rows = part[q * BS : (q + 1) * BS].reshape(NY, 16, 256)
                if h == 0:
                    pz[(mb % 2) * 4 + q, pl.ds((mb // 2) * NY, NY)] = rows
                else:
                    py[:, mb * 4 + q] = rows
            return carry

        lax.fori_loop(0, 4, step, 0)

    def index(sense, h, k):
        long = h // 2 == sense
        return (4 - k if long else 7 - k) * 2 + h % 2

    rings = (
        (pz, (rz_plus, rz_minus), z, (at_z(1), at_z(NZ - 1)), 0),
        (py, (ry_plus, ry_minus), y, (at_y(1), at_y(NY - 1)), 1),
    )

    def hand(ring, sense, h, k, src):
        _, recv, _, devices, r = ring
        i = index(sense, h, k)
        remote(
            src, recv[sense].at[i], ring_send.at[r, sense], ring_recv.at[r, sense, i], devices[sense]
        ).start()

    def owner(ring, sense, k):
        return (ring[2] + (k if sense == 0 else 8 - k)) % 8

    def legs(k):
        for far in (0, 1):
            for p in (0, 1):
                yield 0, (2 * far + p), k - far
                yield 1, (2 - 2 * far + p), k - far

    def begin(ring):
        for sense, h, k in legs(4):
            hand(ring, sense, h, k, ring[0].at[owner(ring, sense, k), pl.ds(h * 4, 4)])

    def take(ring, sense, h, k):
        i = index(sense, h, k)
        arrived(ring[1][sense].at[i], ring_recv.at[ring[4], sense, i])
        return i

    def advance(ring, k):
        for sense, h, kk in legs(k):
            if kk < 2:
                continue
            i = take(ring, sense, h, kk)
            buf = ring[1][sense]
            mine = ring[0][owner(ring, sense, kk - 1), h * 4 : h * 4 + 4]
            buf[i] = (buf[i].astype(F32) + mine.astype(F32)).astype(BF)
            hand(ring, sense, h, kk - 1, buf.at[i])

    def close(ring, mid):
        for h in range(4):
            i = take(ring, 0, h, 1)
            j = take(ring, 1, h, 1)
            mine = ring[0][ring[2], h * 4 : h * 4 + 4]
            mid[h * 4 : h * 4 + 4] = (
                mine.astype(F32) + ring[1][0][i].astype(F32) + ring[1][1][j].astype(F32)
            ).astype(BF)

    def direct_z(o):
        g, device = group_xy(o)
        return remote(z_mid.at[g], z_in.at[gy], far_send.at[0], far_recv.at[0], device)

    def direct_y(o):
        g, device = group_xz(o)
        return remote(y_mid.at[g], y_in.at[gz], far_send.at[1], far_recv.at[1], device)

    def send_direct(direct):
        def step(o, carry):
            direct(o).start()
            return carry

        lax.fori_loop(1, 16, step, 0)

    for i in (1, 2, 3):
        if i > 1:
            hear(0, i)
            hear(1, i)
    apply_operator(0)
    product(0)
    begin(rings[0])
    hear(0, 5)
    tell(0, 7)
    hear(1, 5)
    tell(1, 7)
    advance(rings[0], 4)
    for i in (6, 7):
        hear(0, i)
        hear(1, i)
    apply_operator(1)
    product(1)
    begin(rings[1])
    advance(rings[0], 3)
    advance(rings[0], 2)
    advance(rings[1], 4)
    close(rings[0], z_mid)
    send_direct(direct_z)
    z_in[gy] = z_mid[gy]
    advance(rings[1], 3)
    advance(rings[1], 2)
    close(rings[1], y_mid)
    send_direct(direct_y)
    y_in[gz] = y_mid[gz]

    spot = lax.broadcasted_iota(jnp.int32, (16, 512), 0) + (me % 32) * 16
    on_tile = lax.broadcasted_iota(jnp.int32, (16, 512), 1) == spot

    def column(row):
        spread = jnp.where(on_tile, jnp.broadcast_to(row, (16, 512)), F32(0))
        return jnp.sum(spread, axis=1, keepdims=True)

    def frequency(block):
        at = midx_ref[block]
        high = lax.broadcasted_iota(jnp.int32, (384, 512), 0) == jnp.broadcast_to(at // 128, (384, 512))
        rows = lax.dot_general(
            spec_ref[...], high.astype(F32), (((0,), (0,)), ((), ())),
            precision=lax.Precision.HIGHEST, preferred_element_type=F32,
        )
        low = lax.broadcasted_iota(jnp.int32, (128, 512), 0) == jnp.broadcast_to(at % 128, (128, 512))
        return jnp.sum(jnp.where(low, rows, F32(0)), axis=0, keepdims=True)

    row_freq = frequency(mode)
    row_width = width_ref[mode]
    col_freq = column(frequency(me // 32))
    col_width = column(width_ref[me // 32])
    freq_sum = row_freq + col_freq
    spacing = row_freq - col_freq
    mean_width = 0.5 * (row_width + col_width)
    factor = freq_sum * freq_sum / (4.0 * row_freq * col_freq)
    weight = factor * mean_width / (spacing * spacing + mean_width * mean_width)

    fifteen = pl.ds(0, 15)
    arrived(z_in.at[fifteen], far_recv.at[0])
    arrived(y_in.at[fifteen], far_recv.at[1])
    tile = jnp.concatenate(
        [jnp.sum(z_in[...].astype(F32), axis=0), jnp.sum(y_in[...].astype(F32), axis=0)], axis=1
    )
    tile_ref[...] = tile
    share = jnp.sum(weight * tile * tile, axis=0, keepdims=True)

    for q in range(4):
        s_y[y, q : q + 1, :] = share[:, q * BS : (q + 1) * BS]
    for o in range(1, NY):
        remote(s_y.at[y], s_y.at[y], sum_send.at[0], sum_recv.at[0], at_y(o)).start()
    arrived(s_y.at[pl.ds(0, 7)], sum_recv.at[0])
    s_xz[gz] = jnp.sum(s_y[...], axis=0)
    for o in range(1, 16):
        remote(
            s_xz.at[gz], s_xz.at[gz], sum_send.at[1], sum_recv.at[1], group_xz(o)[1]
        ).start()
    arrived(s_xz.at[fifteen], sum_recv.at[1])
    diff_ref[...] = jnp.sum(s_xz[...], axis=0) * F32(1.0 / 2048)

    for copy in sends:
        copy.wait_send()

    for ref, sem in (
        (z_in.at[fifteen], far_send.at[0]), (y_in.at[fifteen], far_send.at[1]),
        (s_y.at[pl.ds(0, 7)], sum_send.at[0]), (s_xz.at[fifteen], sum_send.at[1]),
        (rz_plus, ring_send.at[0, 0]), (rz_minus, ring_send.at[0, 1]),
        (ry_plus, ring_send.at[1, 0]), (ry_minus, ring_send.at[1, 1]),
    ):
        remote(ref, ref, sem, sem, above).wait_send()


def body(eigvec, operator_blocks, column_blocks, block_mask, spectrum, mode_index, linewidth):
    anywhere = pl.BlockSpec(memory_space=pl.ANY)
    vmem = pl.BlockSpec(memory_space=pltpu.VMEM)
    dma = pltpu.SemaphoreType.DMA
    ring_buffer = pltpu.VMEM((14, 4, 16, 256), BF)
    tile, diff = pl.pallas_call(
        kernel,
        out_shape=(
            jax.ShapeDtypeStruct((16, 512), F32),
            jax.ShapeDtypeStruct((4, BS), F32),
        ),
        in_specs=[anywhere] * 7,
        out_specs=(vmem, vmem),
        scratch_shapes=[
            pltpu.VMEM((2, 11 * BS, 256), BF),
            pltpu.VMEM((3, LB * BS, 512), BF),
            pltpu.VMEM((4, 512, LB * BS), BF),
            pltpu.VMEM((LB, 8, BS, BS), BF),
            pltpu.SMEM((LB, 8), jnp.int32),
            pltpu.SMEM((LB, 8), jnp.int32),
            pltpu.VMEM((384, 128), F32),
            pltpu.VMEM((4, 1, 512), jnp.int32),
            pltpu.VMEM((4, 1, 512), F32),
            pltpu.VMEM((LB, BAND, BS, BS), BF),
            pltpu.VMEM((10, BS, BS), BF),
            pltpu.VMEM((10, BS, BS), BF),
            pltpu.VMEM((10, BS, BS), BF),
            pltpu.VMEM((10, BS, BS), BF),
            pltpu.VMEM((BS, BS), BF),
            pltpu.VMEM((BS, BS), BF),
            pltpu.VMEM((LB, BS, BAND * BS), BF),
            pltpu.VMEM((2, LB * BS, 256), BF),
            pltpu.VMEM((NZ, 16, 16, 256), BF),
            pltpu.VMEM((NY, 16, 16, 256), BF),
            ring_buffer, ring_buffer, ring_buffer, ring_buffer,
            pltpu.VMEM((16, 16, 256), BF),
            pltpu.VMEM((16, 16, 256), BF),
            pltpu.VMEM((16, 16, 256), BF),
            pltpu.VMEM((16, 16, 256), BF),
            pltpu.VMEM((NY, 4, BS), F32),
            pltpu.VMEM((16, 4, BS), F32),
            dma((8,)), dma((5,)), dma((5,)), dma((2,)), dma((2,)), dma((2, 8)), dma((2, 8)),
            dma((2, 2)), dma((2, 2, 14)), dma((2,)), dma((2,)), dma((2,)), dma((2,)),
        ],
        compiler_params=pltpu.CompilerParams(
            collective_id=0, has_side_effects=True, vmem_limit_bytes=40 * 1024 * 1024
        ),
    )(
        *(
            pltpu.with_memory_space_constraint(array, pltpu.HBM)
            for array in (
                eigvec, operator_blocks, column_blocks, block_mask,
                spectrum.reshape(384, 128), mode_index.reshape(4, 1, 512),
                linewidth.reshape(4, 1, 512),
            )
        )
    )
    return tile.T, diff.reshape(512)


def solution(mesh):
    in_specs = (
        P("atoms", "modes"),
        P("atoms", None, None, None),
        P("atoms", None),
        P("atoms", None),
        P(),
        P(),
        P(),
    )
    out_specs = (P("modes", "atoms"), P("modes"))
    return jax.shard_map(body, mesh=mesh, in_specs=in_specs, out_specs=out_specs, check_vma=False)
```

```python
import functools

import jax
import jax.numpy as jnp
from jax import lax
from jax.experimental import pallas as pl
from jax.experimental.pallas import tpu as pltpu
from jax.sharding import PartitionSpec as P

BF = jnp.bfloat16
F32 = jnp.float32
NX, NZ, NY = 2, 8, 8
ATOMS = NX * NZ * NY
REACH = 4
BAND = 2 * REACH + 1
BS = 128
LB = 3
UP = ((0, 7), (0, 8), (1, 6), (1, 7), (1, 8), (2, 5), (2, 6), (2, 7), (2, 8))
DOWN = ((0, 1), (0, 2), (0, 3), (1, 0), (1, 1), (1, 2), (2, 0), (2, 1), (0, 0))


def kernel(
    e_hbm, op_hbm, col_hbm, mask_hbm, spec_hbm, midx_hbm, width_hbm,
    tile_ref, diff_ref,
    ext, others, turned, opv, col_s, mask_s, spec_ref, midx_ref, width_ref,
    dense, up_send, dn_send, lo_blk, hi_blk, lo_far, hi_far,
    bmat, wmat, pz, py, rz_plus, rz_minus, ry_plus, ry_minus, z_mid, y_mid, z_in, y_in,
    s_y, s_xz,
    load_sem, mode_send, mode_recv, blk_send, blk_recv, msg_send, msg_recv, past_send,
    ring_send, ring_recv, far_send, far_recv, sum_send, sum_recv,
):
    me = lax.axis_index("atoms")
    mode = lax.axis_index("modes")
    x_lo, core = mode // 2, mode % 2
    x, z, y = me // (NZ * NY), (me // NY) % NZ, me % NY
    above = ((me + 1) % ATOMS, mode)
    below = ((me + ATOMS - 1) % ATOMS, mode)
    twin = (me, x_lo * 2 + 1 - core)
    across = (me, (1 - x_lo) * 2 + core)
    twin_mode = x_lo * 2 + 1 - core
    across_mode = (1 - x_lo) * 2 + core
    last_mode = (1 - x_lo) * 2 + 1 - core

    def at_y(o):
        return (x * (NZ * NY) + z * NY + (y + o) % NY, mode)

    def at_z(o):
        return (x * (NZ * NY) + ((z + o) % NZ) * NY + y, mode)

    gz = x * NZ + z
    gy = x * NY + y

    def group_xz(o):
        g = (gz + o) % 16
        return g, (g * NY + y, mode)

    def group_xy(o):
        g = (gy + o) % 16
        return g, ((g // NY) * (NZ * NY) + z * NY + g % NY, mode)

    top = (y == NY - 1) & (z == NZ - 1)
    bottom = (y == 0) & (z == 0)
    before_top = (y == NY - 2) & (z == NZ - 1)
    before_bottom = (y == 1) & (z == 0)
    above_across = ((me + 1) % ATOMS, across_mode)
    below_across = ((me + ATOMS - 1) % ATOMS, across_mode)

    def remote(src, dst, ssem, rsem, device):
        return pltpu.make_async_remote_copy(
            src_ref=src, dst_ref=dst, send_sem=ssem, recv_sem=rsem,
            device_id=device, device_id_type=pl.DeviceIdType.MESH,
        )

    loads = (
        (op_hbm, opv), (col_hbm, col_s), (mask_hbm, mask_s),
        (e_hbm.at[:, pl.ds(0, 256)], ext.at[0, pl.ds(REACH * BS, LB * BS)]),
        (e_hbm.at[:, pl.ds(256, 256)], ext.at[1, pl.ds(REACH * BS, LB * BS)]),
        (spec_hbm, spec_ref), (midx_hbm, midx_ref), (width_hbm, width_ref),
    )
    loads = [pltpu.make_async_copy(a, b, load_sem.at[i]) for i, (a, b) in enumerate(loads)]
    for copy in loads:
        copy.start()

    barrier = pltpu.get_barrier_semaphore()

    def greet(device):
        pl.semaphore_signal(
            barrier, inc=1, device_id=device, device_id_type=pl.DeviceIdType.MESH
        )

    for device in (above, below, twin, across):
        greet(device)
    greet(((me + 2) % ATOMS, mode))
    greet(((me + ATOMS - 2) % ATOMS, mode))
    for o in range(1, 16):
        greet(group_xz(o)[1])
        greet(group_xy(o)[1])

    @pl.when(top)
    def _():
        greet(above_across)

    @pl.when(bottom)
    def _():
        greet(below_across)

    extra = jnp.where(top | bottom, 1, 0)

    pl.semaphore_wait(barrier, 36 + extra)

    sends = []
    guarded = []

    def go(*args):
        copy = remote(*args)
        copy.start()
        sends.append(copy)
        return copy

    def arrived(dst, sem):
        remote(dst, dst, sem, sem, above).wait_recv()

    half = pl.ds(core * 5, 5)
    other_half = pl.ds((1 - core) * 5, 5)
    messages = [[(up_send.at[half], lo_blk.at[half])], [(dn_send.at[half], hi_blk.at[half])]]
    for h in range(2):
        lanes = pl.ds(h * 256, 256)
        rows = ext.at[h]
        messages[0] += [
            (e_hbm.at[pl.ds(256, 128), lanes], rows.at[pl.ds(384, 128)]),
            (e_hbm.at[pl.ds(0, 256), lanes], rows.at[pl.ds(128, 256)]),
            (rows.at[pl.ds(384, 128)], rows.at[pl.ds(0, 128)]),
        ]
        messages[1] += [
            (e_hbm.at[pl.ds(0, 128), lanes], rows.at[pl.ds(896, 128)]),
            (e_hbm.at[pl.ds(128, 256), lanes], rows.at[pl.ds(1024, 256)]),
            (rows.at[pl.ds(896, 128)], rows.at[pl.ds(1280, 128)]),
        ]
        if h == 0:
            messages[0].append((up_send.at[8], lo_far))
            messages[1].append((dn_send.at[8], hi_far))

    def message(way, i):
        src, dst = messages[way][i]
        atoms, edge = (above[0], top) if way == 0 else (below[0], bottom)
        to_mode = jnp.where(edge, across_mode, mode) if i == 0 else mode
        if i == 4:
            atoms = (me + (2 if way == 0 else ATOMS - 2)) % ATOMS
        return remote(src, dst, msg_send.at[way, i], msg_recv.at[way, i], (atoms, to_mode)), edge

    def tell(way, i):
        copy, edge = message(way, i)
        if i in (0, 4):
            copy.start()
        else:
            pl.when(jnp.logical_not(edge))(copy.start)

    def tell_past_corner(way):
        edge = before_top if way == 0 else before_bottom
        atoms = (me + (2 if way == 0 else ATOMS - 2)) % ATOMS
        for h in range(2):
            copy = remote(
                messages[way][4 * h + 1][0], messages[way][4 * h + 3][1],
                past_send.at[h], msg_recv.at[way, 4 * h + 3], (atoms, mode),
            )
            pl.when(edge)(copy.start)
            guarded.append((jnp.logical_not(edge), copy))

    def tell_both(i):
        tell(0, i)
        tell(1, i)

    near_rows = pl.ds(pl.multiple_of(jnp.where(bottom, 0, 2 * BS), BS), BS)
    rest_rows = pl.ds(pl.multiple_of(jnp.where(bottom, BS, 0), BS), 2 * BS)
    pieces = (
        (near_rows, pl.ds(0, 512)), (rest_rows, pl.ds(0, 256)), (rest_rows, pl.ds(256, 256))
    )

    def piece(n, p):
        return others.at[n, pieces[p][0], pieces[p][1]]

    def relay(p):
        for way, edge, device in ((0, top, above_across), (1, bottom, below_across)):

            @pl.when(edge)
            def _():
                for h in range(2):
                    if p not in (0, h + 1):
                        continue
                    i = 4 * h + (1 if p == 0 else 2)
                    src = others.at[0, pieces[p][0], pl.ds(h * 256, 256)]
                    remote(
                        src, messages[way][i][1], msg_send.at[way, i], msg_recv.at[way, i], device
                    ).start()

    def hear(way, i):
        arrived(messages[way][i][1], msg_recv.at[way, i])

    for p in range(3):
        go(e_hbm.at[pieces[p][0], pieces[p][1]], piece(0, p), mode_send.at[p], mode_recv.at[p], across)
    go(e_hbm, others.at[1], mode_send.at[3], mode_recv.at[3], twin)
    for way in (0, 1):
        tell_past_corner(way)
    tell_both(1)
    tell_both(5)

    for copy in loads[:3]:
        copy.wait()
    for r in range(LB):
        for d in range(BAND):
            target = (me * LB + r + d - REACH + ATOMS * LB) % (ATOMS * LB)
            slot = jnp.int32(0)
            used = jnp.int32(0)
            for s in range(8):
                hit = col_s[r, s] == target
                slot = jnp.where(hit, s, slot)
                used = jnp.where(hit, mask_s[r, s], used)
            keep = jnp.where(used > 0, F32(1), F32(0)).astype(F32)
            block = (opv[r, slot].astype(F32) * keep).astype(BF)
            dense[r, d] = block
            if (r, d) in UP:
                up_send[UP.index((r, d))] = block
            if (r, d) in DOWN:
                dn_send[DOWN.index((r, d))] = block
    up_send[9] = jnp.zeros((BS, BS), BF)
    dn_send[9] = jnp.zeros((BS, BS), BF)

    tell_both(0)
    tell_both(2)
    tell_both(4)
    corner = top | bottom
    not_corner = jnp.logical_not(corner)
    pl.when(corner)(functools.partial(tell_both, 6))

    def build(r, d, mirror):
        value = mirror.astype(F32).T - dense[r, d].astype(F32)
        bmat[r, :, d * BS : (d + 1) * BS] = value.astype(BF)

    for copy in loads[3:]:
        copy.wait()
    for r in range(LB):
        for c in range(LB):
            d = c - r + REACH
            build(r, d, dense[c, 2 * REACH - d])
    for b in range(LB):
        for h in range(2):
            turned[mode, h * 256 : (h + 1) * 256, b * BS : (b + 1) * BS] = ext[
                h, (REACH + b) * BS : (REACH + b + 1) * BS
            ].T

    def turn_other(n, slot_mode, p):
        for b in range(LB):
            turned[slot_mode, p * BS : (p + 1) * BS, b * BS : (b + 1) * BS] = others[
                n, b * BS : (b + 1) * BS, p * BS : (p + 1) * BS
            ].T

    def hand_over(p):
        arrived(piece(0, p), mode_recv.at[p])
        relay(p)
        go(piece(0, p), piece(2, p), mode_send.at[4 + p], mode_recv.at[4 + p], twin)

    def pass_far(h):
        for way in (0, 1):
            hear(way, 4 * h + 1)
            tell(way, 4 * h + 3)

    def pass_both():
        pass_far(0)
        pass_far(1)

    @pl.when(not_corner)
    def _():
        pass_both()
        tell_both(6)

    hand_over(0)
    hand_over(1)
    hear(0, 0)
    go(lo_blk.at[half], lo_blk.at[half], blk_send.at[0], blk_recv.at[0], twin)
    hear(1, 0)
    go(hi_blk.at[half], hi_blk.at[half], blk_send.at[1], blk_recv.at[1], twin)
    hand_over(2)
    pl.when(corner)(pass_both)
    for p in range(4):
        turn_other(0, across_mode, p)

    arrived(lo_blk.at[other_half], blk_recv.at[0])
    arrived(hi_blk.at[other_half], blk_recv.at[1])
    for k in range(8):
        c, d = UP[k]
        r = d + c - 7
        build(r, c + 1 - r, lo_blk[k])
        c, d = DOWN[k]
        r = d + c - 1
        build(r, c + 7 - r, hi_blk[k])

    arrived(others.at[1], mode_recv.at[3])
    for p in range(4):
        turn_other(1, twin_mode, p)
    for p in range(3):
        arrived(piece(2, p), mode_recv.at[4 + p])
    for p in range(4):
        turn_other(2, last_mode, p)

    hear(0, 4)
    build(0, 0, lo_far[...])
    hear(1, 4)
    build(2, 8, hi_far[...])

    def apply_operator(h):
        for r in range(LB):
            wmat[h, r * BS : (r + 1) * BS, :] = jnp.dot(
                bmat[r], ext[h, r * BS : (r + BAND) * BS], preferred_element_type=F32
            ).astype(BF)

    def product(h):
        def step(mb, carry):
            part = jnp.dot(turned[mb], wmat[h], preferred_element_type=F32).astype(BF)
            for q in range(4):
                rows = part[q * BS : (q + 1) * BS].reshape(NY, 16, 256)
                if h == 0:
                    pz[(mb % 2) * 4 + q, pl.ds((mb // 2) * NY, NY)] = rows
                else:
                    py[:, mb * 4 + q] = rows
            return carry

        for mb in range(4):
            step(mb, 0)

    rings = (
        (pz, (rz_plus, rz_minus), z, at_z, 0),
        (py, (ry_plus, ry_minus), y, at_y, 1),
    )

    def owner(ring, sense, k):
        return (ring[2] + (k if sense == 0 else 8 - k)) % 8

    def hand(ring, sense, i, steps, src):
        device = ring[3](steps if sense == 0 else 8 - steps)
        r = ring[4]
        remote(
            src, ring[1][sense].at[i], ring_send.at[r, sense], ring_recv.at[r, sense, i], device
        ).start()

    def slot(h, k):
        return 2 + (3 - k) * 4 + h

    def quarters():
        for n in range(4):
            yield 0, (n + 2) % 4
            yield 1, n

    def begin(ring):
        for p in range(2):
            for sense in range(2):
                src = ring[0].at[owner(ring, sense, 4), pl.ds((2 * sense + p) * 4, 4)]
                hand(ring, sense, p, 2, src)
        for sense, h in quarters():
            src = ring[0].at[owner(ring, sense, 3), pl.ds(h * 4, 4)]
            hand(ring, sense, slot(h, 3), 1, src)

    def take(ring, sense, i):
        buf = ring[1][sense]
        arrived(buf.at[i], ring_recv.at[ring[4], sense, i])
        return buf[i].astype(F32)

    def advance(ring, k):
        for sense, h in quarters():
            i = slot(h, k)
            mine = ring[0][owner(ring, sense, k - 1), h * 4 : h * 4 + 4]
            total = take(ring, sense, i) + mine.astype(F32)
            if k == 3 and h // 2 == sense:
                total = total + take(ring, sense, h % 2)
            buf = ring[1][sense]
            buf[i] = total.astype(BF)
            hand(ring, sense, slot(h, k - 1), 1, buf.at[i])

    def close(ring, mid):
        for h in range(4):
            mine = ring[0][ring[2], h * 4 : h * 4 + 4].astype(F32)
            both = take(ring, 0, slot(h, 1)) + take(ring, 1, slot(h, 1))
            mid[h * 4 : h * 4 + 4] = (mine + both).astype(BF)

    def direct_z(o):
        g, device = group_xy(o)
        return remote(z_mid.at[g], z_in.at[gy], far_send.at[0], far_recv.at[0], device)

    def direct_y(o):
        g, device = group_xz(o)
        return remote(y_mid.at[g], y_in.at[gz], far_send.at[1], far_recv.at[1], device)

    def send_direct(direct):
        def step(o, carry):
            direct(o).start()
            return carry

        lax.fori_loop(1, 16, step, 0)

    for h in range(2):
        for way in (0, 1):
            hear(way, 4 * h + 2)
            hear(way, 4 * h + 3)
        apply_operator(h)
        product(h)
        begin(rings[h])
    advance(rings[0], 3)
    advance(rings[1], 3)
    advance(rings[0], 2)
    advance(rings[1], 2)
    close(rings[0], z_mid)
    send_direct(direct_z)
    close(rings[1], y_mid)
    send_direct(direct_y)
    z_in[gy] = z_mid[gy]
    y_in[gz] = y_mid[gz]

    spot = lax.broadcasted_iota(jnp.int32, (16, 512), 0) + (me % 32) * 16
    on_tile = lax.broadcasted_iota(jnp.int32, (16, 512), 1) == spot

    def column(row):
        spread = jnp.where(on_tile, jnp.broadcast_to(row, (16, 512)), F32(0))
        return jnp.sum(spread, axis=1, keepdims=True)

    def frequency(block):
        at = midx_ref[block]
        high = lax.broadcasted_iota(jnp.int32, (384, 512), 0) == jnp.broadcast_to(at // 128, (384, 512))
        rows = lax.dot_general(
            spec_ref[...], high.astype(F32), (((0,), (0,)), ((), ())),
            precision=lax.Precision.HIGHEST, preferred_element_type=F32,
        )
        low = lax.broadcasted_iota(jnp.int32, (128, 512), 0) == jnp.broadcast_to(at % 128, (128, 512))
        return jnp.sum(jnp.where(low, rows, F32(0)), axis=0, keepdims=True)

    row_freq = frequency(mode)
    row_width = width_ref[mode]
    col_freq = column(frequency(me // 32))
    col_width = column(width_ref[me // 32])
    freq_sum = row_freq + col_freq
    spacing = row_freq - col_freq
    mean_width = 0.5 * (row_width + col_width)
    factor = freq_sum * freq_sum / (4.0 * row_freq * col_freq)
    weight = factor * mean_width / (spacing * spacing + mean_width * mean_width)

    fifteen = pl.ds(0, 15)
    arrived(z_in.at[fifteen], far_recv.at[0])
    arrived(y_in.at[fifteen], far_recv.at[1])
    tile = jnp.concatenate(
        [jnp.sum(z_in[...].astype(F32), axis=0), jnp.sum(y_in[...].astype(F32), axis=0)], axis=1
    )
    tile_ref[...] = tile
    share = jnp.sum(weight * tile * tile, axis=0, keepdims=True)

    for q in range(4):
        s_y[y, q : q + 1, :] = share[:, q * BS : (q + 1) * BS]
    for o in range(1, NY):
        remote(s_y.at[y], s_y.at[y], sum_send.at[0], sum_recv.at[0], at_y(o)).start()
    arrived(s_y.at[pl.ds(0, 7)], sum_recv.at[0])
    s_xz[gz] = jnp.sum(s_y[...], axis=0)
    for o in range(1, 16):
        remote(
            s_xz.at[gz], s_xz.at[gz], sum_send.at[1], sum_recv.at[1], group_xz(o)[1]
        ).start()
    arrived(s_xz.at[fifteen], sum_recv.at[1])
    diff_ref[...] = jnp.sum(s_xz[...], axis=0) * F32(1.0 / 2048)

    for way in (0, 1):
        for i in range(8):
            copy, edge = message(way, i)
            if i in (3, 7):
                guarded.append((edge, copy))
            else:
                sends.append(copy)
    for copy in sends:
        copy.wait_send()
    for skipped, copy in guarded:
        pl.when(jnp.logical_not(skipped))(copy.wait_send)

    for ref, sem in (
        (z_in.at[fifteen], far_send.at[0]), (y_in.at[fifteen], far_send.at[1]),
        (s_y.at[pl.ds(0, 7)], sum_send.at[0]), (s_xz.at[fifteen], sum_send.at[1]),
        (rz_plus, ring_send.at[0, 0]), (rz_minus, ring_send.at[0, 1]),
        (ry_plus, ring_send.at[1, 0]), (ry_minus, ring_send.at[1, 1]),
    ):
        remote(ref, ref, sem, sem, above).wait_send()


def body(eigvec, operator_blocks, column_blocks, block_mask, spectrum, mode_index, linewidth):
    anywhere = pl.BlockSpec(memory_space=pl.ANY)
    vmem = pl.BlockSpec(memory_space=pltpu.VMEM)
    dma = pltpu.SemaphoreType.DMA
    ring_buffer = pltpu.VMEM((14, 4, 16, 256), BF)
    tile, diff = pl.pallas_call(
        kernel,
        out_shape=(
            jax.ShapeDtypeStruct((16, 512), F32),
            jax.ShapeDtypeStruct((4, BS), F32),
        ),
        in_specs=[anywhere] * 7,
        out_specs=(vmem, vmem),
        scratch_shapes=[
            pltpu.VMEM((2, 11 * BS, 256), BF),
            pltpu.VMEM((3, LB * BS, 512), BF),
            pltpu.VMEM((4, 512, LB * BS), BF),
            pltpu.VMEM((LB, 8, BS, BS), BF),
            pltpu.SMEM((LB, 8), jnp.int32),
            pltpu.SMEM((LB, 8), jnp.int32),
            pltpu.VMEM((384, 128), F32),
            pltpu.VMEM((4, 1, 512), jnp.int32),
            pltpu.VMEM((4, 1, 512), F32),
            pltpu.VMEM((LB, BAND, BS, BS), BF),
            pltpu.VMEM((10, BS, BS), BF),
            pltpu.VMEM((10, BS, BS), BF),
            pltpu.VMEM((10, BS, BS), BF),
            pltpu.VMEM((10, BS, BS), BF),
            pltpu.VMEM((BS, BS), BF),
            pltpu.VMEM((BS, BS), BF),
            pltpu.VMEM((LB, BS, BAND * BS), BF),
            pltpu.VMEM((2, LB * BS, 256), BF),
            pltpu.VMEM((NZ, 16, 16, 256), BF),
            pltpu.VMEM((NY, 16, 16, 256), BF),
            ring_buffer, ring_buffer, ring_buffer, ring_buffer,
            pltpu.VMEM((16, 16, 256), BF),
            pltpu.VMEM((16, 16, 256), BF),
            pltpu.VMEM((16, 16, 256), BF),
            pltpu.VMEM((16, 16, 256), BF),
            pltpu.VMEM((NY, 4, BS), F32),
            pltpu.VMEM((16, 4, BS), F32),
            dma((8,)), dma((7,)), dma((7,)), dma((2,)), dma((2,)), dma((2, 8)), dma((2, 8)), dma((2,)),
            dma((2, 2)), dma((2, 2, 14)), dma((2,)), dma((2,)), dma((2,)), dma((2,)),
        ],
        compiler_params=pltpu.CompilerParams(
            collective_id=0, has_side_effects=True, vmem_limit_bytes=40 * 1024 * 1024
        ),
    )(
        *(
            pltpu.with_memory_space_constraint(array, pltpu.HBM)
            for array in (
                eigvec, operator_blocks, column_blocks, block_mask,
                spectrum.reshape(384, 128), mode_index.reshape(4, 1, 512),
                linewidth.reshape(4, 1, 512),
            )
        )
    )
    return tile.T, diff.reshape(512)


def solution(mesh):
    in_specs = (
        P("atoms", "modes"),
        P("atoms", None, None, None),
        P("atoms", None),
        P("atoms", None),
        P(),
        P(),
        P(),
    )
    out_specs = (P("modes", "atoms"), P("modes"))
    return jax.shard_map(body, mesh=mesh, in_specs=in_specs, out_specs=out_specs, check_vma=False)
```

```python
import functools

import jax
import jax.numpy as jnp
from jax import lax
from jax.experimental import pallas as pl
from jax.experimental.pallas import tpu as pltpu
from jax.sharding import PartitionSpec as P

BF = jnp.bfloat16
F32 = jnp.float32
NX, NZ, NY = 2, 8, 8
ATOMS = NX * NZ * NY
REACH = 4
BAND = 2 * REACH + 1
BS = 128
LB = 3
UP = ((0, 7), (0, 8), (1, 6), (1, 7), (1, 8), (2, 5), (2, 6), (2, 7), (2, 8))
DOWN = ((0, 1), (0, 2), (0, 3), (1, 0), (1, 1), (1, 2), (2, 0), (2, 1), (0, 0))


def kernel(
    e_hbm, op_hbm, col_hbm, mask_hbm, spec_hbm, midx_hbm, width_hbm,
    tile_ref, diff_ref,
    ext, others, turned, opv, col_s, mask_s, spec_ref, midx_ref, width_ref,
    dense, up_send, dn_send, lo_blk, hi_blk, far_out, far_in,
    bmat, wmat, pz, py, rz_plus, rz_minus, ry_plus, ry_minus, z_mid, y_mid, z_in, y_in,
    s_y, s_xz,
    load_sem, mode_send, mode_recv, blk_send, blk_recv, msg_send, msg_recv, past_send,
    ring_send, ring_recv, far_send, far_recv, sum_send, sum_recv,
):
    me = lax.axis_index("atoms")
    mode = lax.axis_index("modes")
    x_lo, core = mode // 2, mode % 2
    x, z, y = me // (NZ * NY), (me // NY) % NZ, me % NY
    above = ((me + 1) % ATOMS, mode)
    below = ((me + ATOMS - 1) % ATOMS, mode)
    twin = (me, x_lo * 2 + 1 - core)
    across = (me, (1 - x_lo) * 2 + core)
    twin_mode = x_lo * 2 + 1 - core
    across_mode = (1 - x_lo) * 2 + core
    last_mode = (1 - x_lo) * 2 + 1 - core

    def at_y(o):
        return (x * (NZ * NY) + z * NY + (y + o) % NY, mode)

    def at_z(o):
        return (x * (NZ * NY) + ((z + o) % NZ) * NY + y, mode)

    gz = x * NZ + z
    gy = x * NY + y

    def group_xz(o):
        g = (gz + o) % 16
        return g, (g * NY + y, mode)

    def group_xy(o):
        g = (gy + o) % 16
        return g, ((g // NY) * (NZ * NY) + z * NY + g % NY, mode)

    top = (y == NY - 1) & (z == NZ - 1)
    bottom = (y == 0) & (z == 0)
    before_top = (y == NY - 2) & (z == NZ - 1)
    before_bottom = (y == 1) & (z == 0)
    above_across = ((me + 1) % ATOMS, across_mode)
    below_across = ((me + ATOMS - 1) % ATOMS, across_mode)
    up_two_across = ((me + 2) % ATOMS, across_mode)
    down_two_across = ((me + ATOMS - 2) % ATOMS, across_mode)

    def remote(src, dst, ssem, rsem, device):
        return pltpu.make_async_remote_copy(
            src_ref=src, dst_ref=dst, send_sem=ssem, recv_sem=rsem,
            device_id=device, device_id_type=pl.DeviceIdType.MESH,
        )

    loads = (
        (op_hbm, opv), (col_hbm, col_s), (mask_hbm, mask_s),
        (e_hbm.at[:, pl.ds(0, 256)], ext.at[0, pl.ds(REACH * BS, LB * BS)]),
        (e_hbm.at[:, pl.ds(256, 256)], ext.at[1, pl.ds(REACH * BS, LB * BS)]),
        (spec_hbm, spec_ref), (midx_hbm, midx_ref), (width_hbm, width_ref),
    )
    loads = [pltpu.make_async_copy(a, b, load_sem.at[i]) for i, (a, b) in enumerate(loads)]
    for copy in loads:
        copy.start()

    barrier = pltpu.get_barrier_semaphore()

    def greet(device):
        pl.semaphore_signal(
            barrier, inc=1, device_id=device, device_id_type=pl.DeviceIdType.MESH
        )

    for device in (above, below, twin, across):
        greet(device)
    greet(((me + 2) % ATOMS, mode))
    greet(((me + ATOMS - 2) % ATOMS, mode))
    for o in range(1, 16):
        greet(group_xz(o)[1])
        greet(group_xy(o)[1])

    @pl.when(top)
    def _():
        greet(above_across)
        greet(up_two_across)

    @pl.when(bottom)
    def _():
        greet(below_across)
        greet(down_two_across)

    pl.when(before_top)(functools.partial(greet, up_two_across))
    pl.when(before_bottom)(functools.partial(greet, down_two_across))

    extra = jnp.where(top | bottom, 2, 0) + jnp.where(before_top | before_bottom, 1, 0)

    pl.semaphore_wait(barrier, 36 + extra)

    sends = []
    guarded = []

    def go(*args):
        copy = remote(*args)
        copy.start()
        sends.append(copy)
        return copy

    def arrived(dst, sem):
        remote(dst, dst, sem, sem, above).wait_recv()

    half = pl.ds(core * 4, 4)
    other_half = pl.ds((1 - core) * 4, 4)
    messages = [[(up_send.at[half], lo_blk.at[half])], [(dn_send.at[half], hi_blk.at[half])]]
    for h in range(2):
        lanes = pl.ds(h * 256, 256)
        rows = ext.at[h]
        messages[0] += [
            (e_hbm.at[pl.ds(256, 128), lanes], rows.at[pl.ds(384, 128)]),
            (e_hbm.at[pl.ds(0, 256), lanes], rows.at[pl.ds(128, 256)]),
            (rows.at[pl.ds(384, 128)], rows.at[pl.ds(0, 128)]),
        ]
        messages[1] += [
            (e_hbm.at[pl.ds(0, 128), lanes], rows.at[pl.ds(896, 128)]),
            (e_hbm.at[pl.ds(128, 256), lanes], rows.at[pl.ds(1024, 256)]),
            (rows.at[pl.ds(896, 128)], rows.at[pl.ds(1280, 128)]),
        ]
        if h == 0:
            messages[0].append(None)
            messages[1].append(None)

    def message(way, i):
        src, dst = messages[way][i]
        atoms, edge = (above[0], top) if way == 0 else (below[0], bottom)
        to_mode = jnp.where(edge, across_mode, mode) if i == 0 else mode
        return remote(src, dst, msg_send.at[way, i], msg_recv.at[way, i], (atoms, to_mode)), edge

    def tell(way, i):
        copy, edge = message(way, i)
        if i == 0:
            copy.start()
        else:
            pl.when(jnp.logical_not(edge))(copy.start)

    def past_corner(way, h):
        rows = pl.ds(2 * BS, BS) if way == 0 else pl.ds(0, BS)
        return remote(
            others.at[0, rows, pl.ds(h * 256, 256)], messages[way][4 * h + 3][1],
            past_send.at[h], msg_recv.at[way, 4 * h + 3], (up_two_across, down_two_across)[way],
        )

    def tell_past_corner(h):
        for way, edge in ((0, before_top), (1, before_bottom)):
            pl.when(edge)(past_corner(way, h).start)

    def tell_both(i):
        tell(0, i)
        tell(1, i)

    near_rows = pl.ds(pl.multiple_of(jnp.where(bottom | before_bottom, 0, 2 * BS), BS), BS)
    rest_rows = pl.ds(pl.multiple_of(jnp.where(bottom | before_bottom, BS, 0), BS), 2 * BS)
    pieces = (
        (near_rows, pl.ds(0, 256)), (near_rows, pl.ds(256, 256)),
        (rest_rows, pl.ds(0, 256)), (rest_rows, pl.ds(256, 256)),
    )

    def piece(n, p):
        return others.at[n, pieces[p][0], pieces[p][1]]

    def relay(p):
        for way, edge, device in ((0, top, above_across), (1, bottom, below_across)):

            @pl.when(edge)
            def _():
                i = (1, 5, 2, 6)[p]
                remote(
                    piece(0, p), messages[way][i][1],
                    msg_send.at[way, i], msg_recv.at[way, i], device,
                ).start()

    def hear(way, i):
        arrived(messages[way][i][1], msg_recv.at[way, i])

    for p in range(4):
        go(e_hbm.at[pieces[p][0], pieces[p][1]], piece(0, p), mode_send.at[p], mode_recv.at[p], across)
    go(e_hbm, others.at[1], mode_send.at[4], mode_recv.at[4], twin)
    tell_both(1)
    tell_both(5)

    for copy in loads[:3]:
        copy.wait()
    for r in range(LB):
        for d in range(BAND):
            target = (me * LB + r + d - REACH + ATOMS * LB) % (ATOMS * LB)
            slot = jnp.int32(0)
            used = jnp.int32(0)
            for s in range(8):
                hit = col_s[r, s] == target
                slot = jnp.where(hit, s, slot)
                used = jnp.where(hit, mask_s[r, s], used)
            keep = jnp.where(used > 0, F32(1), F32(0)).astype(F32)
            block = (opv[r, slot].astype(F32) * keep).astype(BF)
            dense[r, d] = block
            for n, (table, send) in enumerate(((UP, up_send), (DOWN, dn_send))):
                if (r, d) == table[8]:
                    far_out[n] = block
                elif (r, d) in table:
                    send[table.index((r, d))] = block

    tell_both(0)
    two_away = ((me + 2 - 4 * core + ATOMS) % ATOMS, mode)
    go(far_out.at[core], far_in.at[core], blk_send.at[2], blk_recv.at[2], two_away)
    tell_both(2)
    corner = top | bottom
    not_corner = jnp.logical_not(corner)
    pl.when(corner)(functools.partial(tell_both, 6))

    def build(r, d, mirror):
        value = mirror.astype(F32).T - dense[r, d].astype(F32)
        bmat[r, :, d * BS : (d + 1) * BS] = value.astype(BF)

    for copy in loads[3:]:
        copy.wait()
    for r in range(LB):
        for c in range(LB):
            d = c - r + REACH
            build(r, d, dense[c, 2 * REACH - d])
    for b in range(LB):
        for h in range(2):
            turned[mode, h * 256 : (h + 1) * 256, b * BS : (b + 1) * BS] = ext[
                h, (REACH + b) * BS : (REACH + b + 1) * BS
            ].T

    def turn_other(n, slot_mode, p):
        for b in range(LB):
            turned[slot_mode, p * BS : (p + 1) * BS, b * BS : (b + 1) * BS] = others[
                n, b * BS : (b + 1) * BS, p * BS : (p + 1) * BS
            ].T

    def hand_over(p):
        arrived(piece(0, p), mode_recv.at[p])
        relay(p)
        go(piece(0, p), piece(2, p), mode_send.at[5 + p], mode_recv.at[5 + p], twin)

    def pass_far(h):
        for way in (0, 1):
            hear(way, 4 * h + 1)
            tell(way, 4 * h + 3)

    def pass_both():
        pass_far(0)
        pass_far(1)

    for h in range(2):
        hand_over(h)
        tell_past_corner(h)

    @pl.when(not_corner)
    def _():
        pass_both()
        tell_both(6)

    hand_over(2)
    hear(0, 0)
    go(lo_blk.at[half], lo_blk.at[half], blk_send.at[0], blk_recv.at[0], twin)
    hear(1, 0)
    go(hi_blk.at[half], hi_blk.at[half], blk_send.at[1], blk_recv.at[1], twin)
    hand_over(3)
    pl.when(corner)(pass_both)
    arrived(far_in.at[core], blk_recv.at[2])
    go(far_in.at[core], far_in.at[core], blk_send.at[3], blk_recv.at[3], twin)
    for p in range(4):
        turn_other(0, across_mode, p)

    arrived(lo_blk.at[other_half], blk_recv.at[0])
    arrived(hi_blk.at[other_half], blk_recv.at[1])
    for k in range(8):
        c, d = UP[k]
        r = d + c - 7
        build(r, c + 1 - r, lo_blk[k])
        c, d = DOWN[k]
        r = d + c - 1
        build(r, c + 7 - r, hi_blk[k])

    arrived(others.at[1], mode_recv.at[4])
    for p in range(4):
        turn_other(1, twin_mode, p)
    for p in range(4):
        arrived(piece(2, p), mode_recv.at[5 + p])
    for p in range(4):
        turn_other(2, last_mode, p)

    arrived(far_in.at[1 - core], blk_recv.at[3])
    build(0, 0, far_in[0])
    build(2, 8, far_in[1])

    def apply_operator(h):
        for r in range(LB):
            wmat[h, r * BS : (r + 1) * BS, :] = jnp.dot(
                bmat[r], ext[h, r * BS : (r + BAND) * BS], preferred_element_type=F32
            ).astype(BF)

    def product(h):
        def step(mb, carry):
            part = jnp.dot(turned[mb], wmat[h], preferred_element_type=F32).astype(BF)
            for q in range(4):
                rows = part[q * BS : (q + 1) * BS].reshape(NY, 16, 256)
                if h == 0:
                    pz[(mb % 2) * 4 + q, pl.ds((mb // 2) * NY, NY)] = rows
                else:
                    py[:, mb * 4 + q] = rows
            return carry

        for mb in range(4):
            step(mb, 0)

    rings = (
        (pz, (rz_plus, rz_minus), z, at_z, 0),
        (py, (ry_plus, ry_minus), y, at_y, 1),
    )

    def owner(ring, sense, k):
        return (ring[2] + (k if sense == 0 else 8 - k)) % 8

    def hand(ring, sense, i, steps, src):
        device = ring[3](steps if sense == 0 else 8 - steps)
        r = ring[4]
        remote(
            src, ring[1][sense].at[i], ring_send.at[r, sense], ring_recv.at[r, sense, i], device
        ).start()

    def slot(h, k):
        return 2 + (3 - k) * 4 + h

    def quarters():
        for n in range(4):
            yield 0, (n + 2) % 4
            yield 1, n

    def begin(ring):
        for p in range(2):
            for sense in range(2):
                src = ring[0].at[owner(ring, sense, 4), pl.ds((2 * sense + p) * 4, 4)]
                hand(ring, sense, p, 2, src)
        for sense, h in quarters():
            src = ring[0].at[owner(ring, sense, 3), pl.ds(h * 4, 4)]
            hand(ring, sense, slot(h, 3), 1, src)

    def take(ring, sense, i):
        buf = ring[1][sense]
        arrived(buf.at[i], ring_recv.at[ring[4], sense, i])
        return buf[i]

    def advance(ring, k):
        for sense, h in quarters():
            i = slot(h, k)
            mine = ring[0][owner(ring, sense, k - 1), h * 4 : h * 4 + 4]
            buf = ring[1][sense]
            if k == 3 and h // 2 == sense:
                buf[i] = (
                    take(ring, sense, i).astype(F32) + mine.astype(F32)
                    + take(ring, sense, h % 2).astype(F32)
                ).astype(BF)
            else:
                buf[i] = take(ring, sense, i) + mine
            hand(ring, sense, slot(h, k - 1), 1, buf.at[i])

    def close(ring, mid):
        for h in range(4):
            mine = ring[0][ring[2], h * 4 : h * 4 + 4].astype(F32)
            both = take(ring, 0, slot(h, 1)).astype(F32) + take(ring, 1, slot(h, 1)).astype(F32)
            mid[h * 4 : h * 4 + 4] = (mine + both).astype(BF)

    def direct_z(o):
        g, device = group_xy(o)
        return remote(z_mid.at[g], z_in.at[gy], far_send.at[0], far_recv.at[0], device)

    def direct_y(o):
        g, device = group_xz(o)
        return remote(y_mid.at[g], y_in.at[gz], far_send.at[1], far_recv.at[1], device)

    def send_direct(direct):
        def step(o, carry):
            direct(o).start()
            return carry

        lax.fori_loop(1, 16, step, 0)

    hear(0, 2)
    hear(1, 2)
    hear(0, 3)
    hear(1, 3)
    apply_operator(0)
    product(0)
    begin(rings[0])
    hear(0, 6)
    hear(1, 6)
    hear(0, 7)
    hear(1, 7)
    apply_operator(1)
    product(1)
    begin(rings[1])
    advance(rings[0], 3)
    advance(rings[1], 3)
    advance(rings[0], 2)
    advance(rings[1], 2)
    close(rings[0], z_mid)
    send_direct(direct_z)
    close(rings[1], y_mid)
    send_direct(direct_y)
    z_in[gy] = z_mid[gy]
    y_in[gz] = y_mid[gz]

    spot = lax.broadcasted_iota(jnp.int32, (16, 512), 0) + (me % 32) * 16
    on_tile = lax.broadcasted_iota(jnp.int32, (16, 512), 1) == spot

    def column(row):
        spread = jnp.where(on_tile, jnp.broadcast_to(row, (16, 512)), F32(0))
        return jnp.sum(spread, axis=1, keepdims=True)

    def frequency(block):
        at = midx_ref[block]
        high = lax.broadcasted_iota(jnp.int32, (384, 512), 0) == jnp.broadcast_to(at // 128, (384, 512))
        rows = lax.dot_general(
            spec_ref[...], high.astype(F32), (((0,), (0,)), ((), ())),
            precision=lax.Precision.HIGHEST, preferred_element_type=F32,
        )
        low = lax.broadcasted_iota(jnp.int32, (128, 512), 0) == jnp.broadcast_to(at % 128, (128, 512))
        return jnp.sum(jnp.where(low, rows, F32(0)), axis=0, keepdims=True)

    row_freq = frequency(mode)
    row_width = width_ref[mode]
    col_freq = column(frequency(me // 32))
    col_width = column(width_ref[me // 32])
    freq_sum = row_freq + col_freq
    spacing = row_freq - col_freq
    mean_width = 0.5 * (row_width + col_width)
    factor = freq_sum * freq_sum / (4.0 * row_freq * col_freq)
    weight = factor * mean_width / (spacing * spacing + mean_width * mean_width)

    fifteen = pl.ds(0, 15)
    arrived(z_in.at[fifteen], far_recv.at[0])
    arrived(y_in.at[fifteen], far_recv.at[1])
    tile = jnp.concatenate(
        [jnp.sum(z_in[...].astype(F32), axis=0), jnp.sum(y_in[...].astype(F32), axis=0)], axis=1
    )
    tile_ref[...] = tile
    share = jnp.sum(weight * tile * tile, axis=0, keepdims=True)

    for q in range(4):
        s_y[y, q : q + 1, :] = share[:, q * BS : (q + 1) * BS]
    for o in range(1, NY):
        remote(s_y.at[y], s_y.at[y], sum_send.at[0], sum_recv.at[0], at_y(o)).start()
    arrived(s_y.at[pl.ds(0, 7)], sum_recv.at[0])
    s_xz[gz] = jnp.sum(s_y[...], axis=0)
    for o in range(1, 16):
        remote(
            s_xz.at[gz], s_xz.at[gz], sum_send.at[1], sum_recv.at[1], group_xz(o)[1]
        ).start()
    arrived(s_xz.at[fifteen], sum_recv.at[1])
    diff_ref[...] = jnp.sum(s_xz[...], axis=0) * F32(1.0 / 2048)

    for way in (0, 1):
        for i in (0, 1, 2, 3, 5, 6, 7):
            copy, edge = message(way, i)
            if i in (3, 7):
                guarded.append((edge, copy))
            else:
                sends.append(copy)
        for h in range(2):
            edge = (before_top, before_bottom)[way]
            guarded.append((jnp.logical_not(edge), past_corner(way, h)))
    for copy in sends:
        copy.wait_send()
    for skipped, copy in guarded:
        pl.when(jnp.logical_not(skipped))(copy.wait_send)

    for ref, sem in (
        (z_in.at[fifteen], far_send.at[0]), (y_in.at[fifteen], far_send.at[1]),
        (s_y.at[pl.ds(0, 7)], sum_send.at[0]), (s_xz.at[fifteen], sum_send.at[1]),
        (rz_plus, ring_send.at[0, 0]), (rz_minus, ring_send.at[0, 1]),
        (ry_plus, ring_send.at[1, 0]), (ry_minus, ring_send.at[1, 1]),
    ):
        remote(ref, ref, sem, sem, above).wait_send()


def body(eigvec, operator_blocks, column_blocks, block_mask, spectrum, mode_index, linewidth):
    anywhere = pl.BlockSpec(memory_space=pl.ANY)
    vmem = pl.BlockSpec(memory_space=pltpu.VMEM)
    dma = pltpu.SemaphoreType.DMA
    ring_buffer = pltpu.VMEM((14, 4, 16, 256), BF)
    tile, diff = pl.pallas_call(
        kernel,
        out_shape=(
            jax.ShapeDtypeStruct((16, 512), F32),
            jax.ShapeDtypeStruct((4, BS), F32),
        ),
        in_specs=[anywhere] * 7,
        out_specs=(vmem, vmem),
        scratch_shapes=[
            pltpu.VMEM((2, 11 * BS, 256), BF),
            pltpu.VMEM((3, LB * BS, 512), BF),
            pltpu.VMEM((4, 512, LB * BS), BF),
            pltpu.VMEM((LB, 8, BS, BS), BF),
            pltpu.SMEM((LB, 8), jnp.int32),
            pltpu.SMEM((LB, 8), jnp.int32),
            pltpu.VMEM((384, 128), F32),
            pltpu.VMEM((4, 1, 512), jnp.int32),
            pltpu.VMEM((4, 1, 512), F32),
            pltpu.VMEM((LB, BAND, BS, BS), BF),
            pltpu.VMEM((8, BS, BS), BF),
            pltpu.VMEM((8, BS, BS), BF),
            pltpu.VMEM((8, BS, BS), BF),
            pltpu.VMEM((8, BS, BS), BF),
            pltpu.VMEM((2, BS, BS), BF),
            pltpu.VMEM((2, BS, BS), BF),
            pltpu.VMEM((LB, BS, BAND * BS), BF),
            pltpu.VMEM((2, LB * BS, 256), BF),
            pltpu.VMEM((NZ, 16, 16, 256), BF),
            pltpu.VMEM((NY, 16, 16, 256), BF),
            ring_buffer, ring_buffer, ring_buffer, ring_buffer,
            pltpu.VMEM((16, 16, 256), BF),
            pltpu.VMEM((16, 16, 256), BF),
            pltpu.VMEM((16, 16, 256), BF),
            pltpu.VMEM((16, 16, 256), BF),
            pltpu.VMEM((NY, 4, BS), F32),
            pltpu.VMEM((16, 4, BS), F32),
            dma((8,)), dma((9,)), dma((9,)), dma((4,)), dma((4,)), dma((2, 8)), dma((2, 8)), dma((2,)),
            dma((2, 2)), dma((2, 2, 14)), dma((2,)), dma((2,)), dma((2,)), dma((2,)),
        ],
        compiler_params=pltpu.CompilerParams(
            collective_id=0, has_side_effects=True, vmem_limit_bytes=40 * 1024 * 1024
        ),
    )(
        *(
            pltpu.with_memory_space_constraint(array, pltpu.HBM)
            for array in (
                eigvec, operator_blocks, column_blocks, block_mask,
                spectrum.reshape(384, 128), mode_index.reshape(4, 1, 512),
                linewidth.reshape(4, 1, 512),
            )
        )
    )
    return tile.T, diff.reshape(512)


def solution(mesh):
    in_specs = (
        P("atoms", "modes"),
        P("atoms", None, None, None),
        P("atoms", None),
        P("atoms", None),
        P(),
        P(),
        P(),
    )
    out_specs = (P("modes", "atoms"), P("modes"))
    return jax.shard_map(body, mesh=mesh, in_specs=in_specs, out_specs=out_specs, check_vma=False)
```

```python
import functools

import jax
import jax.numpy as jnp
from jax import lax
from jax.experimental import pallas as pl
from jax.experimental.pallas import tpu as pltpu
from jax.sharding import PartitionSpec as P

BF = jnp.bfloat16
F32 = jnp.float32
NX, NZ, NY = 2, 8, 8
ATOMS = NX * NZ * NY
REACH = 4
BAND = 2 * REACH + 1
BS = 128
LB = 3
UP = ((0, 7), (0, 8), (1, 6), (1, 7), (1, 8), (2, 5), (2, 6), (2, 7), (2, 8))
DOWN = ((0, 1), (0, 2), (0, 3), (1, 0), (1, 1), (1, 2), (2, 0), (2, 1), (0, 0))


def kernel(
    e_hbm, op_hbm, col_hbm, mask_hbm, spec_hbm, midx_hbm, width_hbm,
    tile_ref, diff_ref,
    ext, others, turned, opv, col_s, mask_s, spec_ref, midx_ref, width_ref,
    dense, up_send, dn_send, lo_blk, hi_blk, far_out, far_in,
    bmat, wmat, pz, py, rz_plus, rz_minus, ry_plus, ry_minus, z_mid, y_mid, z_in, y_in,
    s_y, s_xz,
    load_sem, mode_send, mode_recv, blk_send, blk_recv, msg_send, msg_recv, past_send,
    ring_send, ring_recv, far_send, far_recv, sum_send, sum_recv,
):
    me = lax.axis_index("atoms")
    mode = lax.axis_index("modes")
    x_lo, core = mode // 2, mode % 2
    x, z, y = me // (NZ * NY), (me // NY) % NZ, me % NY
    above = ((me + 1) % ATOMS, mode)
    below = ((me + ATOMS - 1) % ATOMS, mode)
    twin = (me, x_lo * 2 + 1 - core)
    across = (me, (1 - x_lo) * 2 + core)
    twin_mode = x_lo * 2 + 1 - core
    across_mode = (1 - x_lo) * 2 + core
    last_mode = (1 - x_lo) * 2 + 1 - core

    def at_y(o):
        return (x * (NZ * NY) + z * NY + (y + o) % NY, mode)

    def at_z(o):
        return (x * (NZ * NY) + ((z + o) % NZ) * NY + y, mode)

    gz = x * NZ + z
    gy = x * NY + y

    def group_xz(o):
        g = (gz + o) % 16
        return g, (g * NY + y, mode)

    def group_xy(o):
        g = (gy + o) % 16
        return g, ((g // NY) * (NZ * NY) + z * NY + g % NY, mode)

    top = (y == NY - 1) & (z == NZ - 1)
    bottom = (y == 0) & (z == 0)
    before_top = (y == NY - 2) & (z == NZ - 1)
    before_bottom = (y == 1) & (z == 0)
    above_across = ((me + 1) % ATOMS, across_mode)
    below_across = ((me + ATOMS - 1) % ATOMS, across_mode)
    up_two_across = ((me + 2) % ATOMS, across_mode)
    down_two_across = ((me + ATOMS - 2) % ATOMS, across_mode)

    def remote(src, dst, ssem, rsem, device):
        return pltpu.make_async_remote_copy(
            src_ref=src, dst_ref=dst, send_sem=ssem, recv_sem=rsem,
            device_id=device, device_id_type=pl.DeviceIdType.MESH,
        )

    loads = (
        (op_hbm, opv), (col_hbm, col_s), (mask_hbm, mask_s),
        (e_hbm.at[:, pl.ds(0, 256)], ext.at[0, pl.ds(REACH * BS, LB * BS)]),
        (e_hbm.at[:, pl.ds(256, 256)], ext.at[1, pl.ds(REACH * BS, LB * BS)]),
        (spec_hbm, spec_ref), (midx_hbm, midx_ref), (width_hbm, width_ref),
    )
    loads = [pltpu.make_async_copy(a, b, load_sem.at[i]) for i, (a, b) in enumerate(loads)]
    for copy in loads:
        copy.start()

    barrier = pltpu.get_barrier_semaphore()

    def greet(device):
        pl.semaphore_signal(
            barrier, inc=1, device_id=device, device_id_type=pl.DeviceIdType.MESH
        )

    for device in (above, below, twin, across):
        greet(device)
    greet(((me + 2) % ATOMS, mode))
    greet(((me + ATOMS - 2) % ATOMS, mode))
    for o in range(1, 16):
        greet(group_xz(o)[1])
        greet(group_xy(o)[1])

    @pl.when(top)
    def _():
        greet(above_across)
        greet(up_two_across)

    @pl.when(bottom)
    def _():
        greet(below_across)
        greet(down_two_across)

    pl.when(before_top)(functools.partial(greet, up_two_across))
    pl.when(before_bottom)(functools.partial(greet, down_two_across))

    extra = jnp.where(top | bottom, 2, 0) + jnp.where(before_top | before_bottom, 1, 0)

    pl.semaphore_wait(barrier, 36 + extra)

    sends = []
    guarded = []

    def go(*args):
        copy = remote(*args)
        copy.start()
        sends.append(copy)
        return copy

    def arrived(dst, sem):
        remote(dst, dst, sem, sem, above).wait_recv()

    half = pl.ds(core * 4, 4)
    other_half = pl.ds((1 - core) * 4, 4)
    messages = [[(up_send.at[half], lo_blk.at[half])], [(dn_send.at[half], hi_blk.at[half])]]
    for h in range(2):
        lanes = pl.ds(h * 256, 256)
        rows = ext.at[h]
        messages[0] += [
            (e_hbm.at[pl.ds(256, 128), lanes], rows.at[pl.ds(384, 128)]),
            (e_hbm.at[pl.ds(0, 256), lanes], rows.at[pl.ds(128, 256)]),
            (rows.at[pl.ds(384, 128)], rows.at[pl.ds(0, 128)]),
        ]
        messages[1] += [
            (e_hbm.at[pl.ds(0, 128), lanes], rows.at[pl.ds(896, 128)]),
            (e_hbm.at[pl.ds(128, 256), lanes], rows.at[pl.ds(1024, 256)]),
            (rows.at[pl.ds(896, 128)], rows.at[pl.ds(1280, 128)]),
        ]
        if h == 0:
            messages[0].append(None)
            messages[1].append(None)

    def message(way, i):
        src, dst = messages[way][i]
        atoms, edge = (above[0], top) if way == 0 else (below[0], bottom)
        to_mode = jnp.where(edge, across_mode, mode) if i == 0 else mode
        return remote(src, dst, msg_send.at[way, i], msg_recv.at[way, i], (atoms, to_mode)), edge

    def tell(way, i):
        copy, edge = message(way, i)
        if i == 0:
            copy.start()
        else:
            pl.when(jnp.logical_not(edge))(copy.start)

    def past_corner(way, h):
        rows = pl.ds(2 * BS, BS) if way == 0 else pl.ds(0, BS)
        return remote(
            others.at[0, rows, pl.ds(h * 256, 256)], messages[way][4 * h + 3][1],
            past_send.at[h], msg_recv.at[way, 4 * h + 3], (up_two_across, down_two_across)[way],
        )

    def tell_past_corner(h):
        for way, edge in ((0, before_top), (1, before_bottom)):
            pl.when(edge)(past_corner(way, h).start)

    def tell_both(i):
        tell(0, i)
        tell(1, i)

    near_rows = pl.ds(pl.multiple_of(jnp.where(bottom | before_bottom, 0, 2 * BS), BS), BS)
    rest_rows = pl.ds(pl.multiple_of(jnp.where(bottom | before_bottom, BS, 0), BS), 2 * BS)
    pieces = (
        (near_rows, pl.ds(0, 256)), (near_rows, pl.ds(256, 256)),
        (rest_rows, pl.ds(0, 256)), (rest_rows, pl.ds(256, 256)),
    )

    def piece(n, p):
        return others.at[n, pieces[p][0], pieces[p][1]]

    def relay(p):
        for way, edge, device in ((0, top, above_across), (1, bottom, below_across)):

            @pl.when(edge)
            def _():
                i = (1, 5, 2, 6)[p]
                remote(
                    piece(0, p), messages[way][i][1],
                    msg_send.at[way, i], msg_recv.at[way, i], device,
                ).start()

    def hear(way, i):
        arrived(messages[way][i][1], msg_recv.at[way, i])

    for p in range(4):
        go(e_hbm.at[pieces[p][0], pieces[p][1]], piece(0, p), mode_send.at[p], mode_recv.at[p], across)
    go(e_hbm, others.at[1], mode_send.at[4], mode_recv.at[4], twin)
    tell_both(1)
    tell_both(5)

    for copy in loads[:3]:
        copy.wait()
    for r in range(LB):
        for d in range(BAND):
            target = (me * LB + r + d - REACH + ATOMS * LB) % (ATOMS * LB)
            slot = jnp.int32(0)
            used = jnp.int32(0)
            for s in range(8):
                hit = col_s[r, s] == target
                slot = jnp.where(hit, s, slot)
                used = jnp.where(hit, mask_s[r, s], used)
            keep = jnp.where(used > 0, F32(1), F32(0)).astype(F32)
            block = (opv[r, slot].astype(F32) * keep).astype(BF)
            dense[r, d] = block
            for n, (table, send) in enumerate(((UP, up_send), (DOWN, dn_send))):
                if (r, d) == table[8]:
                    far_out[n] = block
                elif (r, d) in table:
                    send[table.index((r, d))] = block

    tell_both(0)
    two_away = ((me + 2 - 4 * core + ATOMS) % ATOMS, mode)
    go(far_out.at[core], far_in.at[core], blk_send.at[2], blk_recv.at[2], two_away)
    tell_both(2)
    corner = top | bottom
    not_corner = jnp.logical_not(corner)
    pl.when(corner)(functools.partial(tell_both, 6))

    def build(r, d, mirror):
        value = mirror.astype(F32).T - dense[r, d].astype(F32)
        bmat[r, :, d * BS : (d + 1) * BS] = value.astype(BF)

    for copy in loads[3:]:
        copy.wait()
    for r in range(LB):
        for c in range(LB):
            d = c - r + REACH
            build(r, d, dense[c, 2 * REACH - d])
    for b in range(LB):
        for h in range(2):
            turned[mode, h * 256 : (h + 1) * 256, b * BS : (b + 1) * BS] = ext[
                h, (REACH + b) * BS : (REACH + b + 1) * BS
            ].T

    def turn_other(n, slot_mode, p):
        for b in range(LB):
            turned[slot_mode, p * BS : (p + 1) * BS, b * BS : (b + 1) * BS] = others[
                n, b * BS : (b + 1) * BS, p * BS : (p + 1) * BS
            ].T

    def hand_over(p):
        arrived(piece(0, p), mode_recv.at[p])
        relay(p)
        go(piece(0, p), piece(2, p), mode_send.at[5 + p], mode_recv.at[5 + p], twin)

    def pass_far(h):
        for way in (0, 1):
            hear(way, 4 * h + 1)
            tell(way, 4 * h + 3)

    def pass_both():
        pass_far(0)
        pass_far(1)

    for h in range(2):
        hand_over(h)
        tell_past_corner(h)

    @pl.when(not_corner)
    def _():
        pass_both()
        tell_both(6)

    hand_over(2)
    hear(0, 0)
    go(lo_blk.at[half], lo_blk.at[half], blk_send.at[0], blk_recv.at[0], twin)
    hear(1, 0)
    go(hi_blk.at[half], hi_blk.at[half], blk_send.at[1], blk_recv.at[1], twin)
    hand_over(3)
    pl.when(corner)(pass_both)
    arrived(far_in.at[core], blk_recv.at[2])
    go(far_in.at[core], far_in.at[core], blk_send.at[3], blk_recv.at[3], twin)
    for p in range(4):
        turn_other(0, across_mode, p)

    arrived(lo_blk.at[other_half], blk_recv.at[0])
    arrived(hi_blk.at[other_half], blk_recv.at[1])
    for k in range(8):
        c, d = UP[k]
        r = d + c - 7
        build(r, c + 1 - r, lo_blk[k])
        c, d = DOWN[k]
        r = d + c - 1
        build(r, c + 7 - r, hi_blk[k])

    arrived(others.at[1], mode_recv.at[4])
    for p in range(4):
        turn_other(1, twin_mode, p)
    for p in range(4):
        arrived(piece(2, p), mode_recv.at[5 + p])
    for p in range(4):
        turn_other(2, last_mode, p)

    arrived(far_in.at[1 - core], blk_recv.at[3])
    build(0, 0, far_in[0])
    build(2, 8, far_in[1])

    def apply_operator(h):
        for r in range(LB):
            wmat[h, r * BS : (r + 1) * BS, :] = jnp.dot(
                bmat[r], ext[h, r * BS : (r + BAND) * BS], preferred_element_type=F32
            ).astype(BF)

    def product(h):
        def step(mb, carry):
            part = jnp.dot(turned[mb], wmat[h], preferred_element_type=F32).astype(BF)
            for q in range(4):
                rows = part[q * BS : (q + 1) * BS].reshape(NY, 16, 256)
                if h == 0:
                    pz[(mb % 2) * 4 + q, pl.ds((mb // 2) * NY, NY)] = rows
                else:
                    py[:, mb * 4 + q] = rows
            return carry

        for mb in range(4):
            step(mb, 0)

    rings = (
        (pz, (rz_plus, rz_minus), z, at_z, 0),
        (py, (ry_plus, ry_minus), y, at_y, 1),
    )

    def owner(ring, sense, k):
        return (ring[2] + (k if sense == 0 else 8 - k)) % 8

    def hand(ring, sense, i, steps, src):
        device = ring[3](steps if sense == 0 else 8 - steps)
        r = ring[4]
        remote(
            src, ring[1][sense].at[i], ring_send.at[r, sense], ring_recv.at[r, sense, i], device
        ).start()

    def slot(h, k):
        return 2 + (3 - k) * 4 + h

    def quarters():
        for n in range(4):
            yield 0, (n + 2) % 4
            yield 1, n

    def begin(ring):
        for n, (sense, h) in enumerate(quarters()):
            src = ring[0].at[owner(ring, sense, 3), pl.ds(h * 4, 4)]
            hand(ring, sense, slot(h, 3), 1, src)
            if n != 3:
                continue
            for p in range(2):
                for way in range(2):
                    far = ring[0].at[owner(ring, way, 4), pl.ds((2 * way + p) * 4, 4)]
                    hand(ring, way, p, 2, far)

    def take(ring, sense, i):
        buf = ring[1][sense]
        arrived(buf.at[i], ring_recv.at[ring[4], sense, i])
        return buf[i]

    def advance(ring, k):
        for sense, h in quarters():
            i = slot(h, k)
            mine = ring[0][owner(ring, sense, k - 1), h * 4 : h * 4 + 4]
            buf = ring[1][sense]
            if k == 3 and h // 2 == sense:
                buf[i] = (
                    take(ring, sense, i).astype(F32) + mine.astype(F32)
                    + take(ring, sense, h % 2).astype(F32)
                ).astype(BF)
            else:
                buf[i] = take(ring, sense, i) + mine
            hand(ring, sense, slot(h, k - 1), 1, buf.at[i])

    def close(ring, mid):
        for h in range(4):
            mine = ring[0][ring[2], h * 4 : h * 4 + 4].astype(F32)
            both = take(ring, 0, slot(h, 1)).astype(F32) + take(ring, 1, slot(h, 1)).astype(F32)
            mid[h * 4 : h * 4 + 4] = (mine + both).astype(BF)

    def direct_z(o):
        g, device = group_xy(o)
        return remote(z_mid.at[g], z_in.at[gy], far_send.at[0], far_recv.at[0], device)

    def direct_y(o):
        g, device = group_xz(o)
        return remote(y_mid.at[g], y_in.at[gz], far_send.at[1], far_recv.at[1], device)

    def send_direct(direct):
        def step(o, carry):
            direct(o).start()
            return carry

        lax.fori_loop(1, 16, step, 0)

    hear(0, 2)
    hear(1, 2)
    hear(0, 3)
    hear(1, 3)
    apply_operator(0)
    product(0)
    begin(rings[0])
    hear(0, 6)
    hear(1, 6)
    hear(0, 7)
    hear(1, 7)
    apply_operator(1)
    product(1)
    begin(rings[1])
    advance(rings[0], 3)
    advance(rings[1], 3)
    advance(rings[0], 2)
    advance(rings[1], 2)
    close(rings[0], z_mid)
    send_direct(direct_z)
    close(rings[1], y_mid)
    send_direct(direct_y)
    z_in[gy] = z_mid[gy]
    y_in[gz] = y_mid[gz]

    spot = lax.broadcasted_iota(jnp.int32, (16, 512), 0) + (me % 32) * 16
    on_tile = lax.broadcasted_iota(jnp.int32, (16, 512), 1) == spot

    def column(row):
        spread = jnp.where(on_tile, jnp.broadcast_to(row, (16, 512)), F32(0))
        return jnp.sum(spread, axis=1, keepdims=True)

    def frequency(block):
        at = midx_ref[block]
        high = lax.broadcasted_iota(jnp.int32, (384, 512), 0) == jnp.broadcast_to(at // 128, (384, 512))
        rows = lax.dot_general(
            spec_ref[...], high.astype(F32), (((0,), (0,)), ((), ())),
            precision=lax.Precision.HIGHEST, preferred_element_type=F32,
        )
        low = lax.broadcasted_iota(jnp.int32, (128, 512), 0) == jnp.broadcast_to(at % 128, (128, 512))
        return jnp.sum(jnp.where(low, rows, F32(0)), axis=0, keepdims=True)

    row_freq = frequency(mode)
    row_width = width_ref[mode]
    col_freq = column(frequency(me // 32))
    col_width = column(width_ref[me // 32])
    freq_sum = row_freq + col_freq
    spacing = row_freq - col_freq
    mean_width = 0.5 * (row_width + col_width)
    factor = freq_sum * freq_sum / (4.0 * row_freq * col_freq)
    weight = factor * mean_width / (spacing * spacing + mean_width * mean_width)

    fifteen = pl.ds(0, 15)
    arrived(z_in.at[fifteen], far_recv.at[0])
    arrived(y_in.at[fifteen], far_recv.at[1])
    tile = jnp.concatenate(
        [jnp.sum(z_in[...].astype(F32), axis=0), jnp.sum(y_in[...].astype(F32), axis=0)], axis=1
    )
    tile_ref[...] = tile
    share = jnp.sum(weight * tile * tile, axis=0, keepdims=True)

    for q in range(4):
        s_y[y, q : q + 1, :] = share[:, q * BS : (q + 1) * BS]
    for o in range(1, NY):
        remote(s_y.at[y], s_y.at[y], sum_send.at[0], sum_recv.at[0], at_y(o)).start()
    arrived(s_y.at[pl.ds(0, 7)], sum_recv.at[0])
    s_xz[gz] = jnp.sum(s_y[...], axis=0)
    for o in range(1, 16):
        remote(
            s_xz.at[gz], s_xz.at[gz], sum_send.at[1], sum_recv.at[1], group_xz(o)[1]
        ).start()
    arrived(s_xz.at[fifteen], sum_recv.at[1])
    diff_ref[...] = jnp.sum(s_xz[...], axis=0) * F32(1.0 / 2048)

    for way in (0, 1):
        for i in (0, 1, 2, 3, 5, 6, 7):
            copy, edge = message(way, i)
            if i in (3, 7):
                guarded.append((edge, copy))
            else:
                sends.append(copy)
        for h in range(2):
            edge = (before_top, before_bottom)[way]
            guarded.append((jnp.logical_not(edge), past_corner(way, h)))
    for copy in sends:
        copy.wait_send()
    for skipped, copy in guarded:
        pl.when(jnp.logical_not(skipped))(copy.wait_send)

    for ref, sem in (
        (z_in.at[fifteen], far_send.at[0]), (y_in.at[fifteen], far_send.at[1]),
        (s_y.at[pl.ds(0, 7)], sum_send.at[0]), (s_xz.at[fifteen], sum_send.at[1]),
        (rz_plus, ring_send.at[0, 0]), (rz_minus, ring_send.at[0, 1]),
        (ry_plus, ring_send.at[1, 0]), (ry_minus, ring_send.at[1, 1]),
    ):
        remote(ref, ref, sem, sem, above).wait_send()


def body(eigvec, operator_blocks, column_blocks, block_mask, spectrum, mode_index, linewidth):
    anywhere = pl.BlockSpec(memory_space=pl.ANY)
    vmem = pl.BlockSpec(memory_space=pltpu.VMEM)
    dma = pltpu.SemaphoreType.DMA
    ring_buffer = pltpu.VMEM((14, 4, 16, 256), BF)
    tile, diff = pl.pallas_call(
        kernel,
        out_shape=(
            jax.ShapeDtypeStruct((16, 512), F32),
            jax.ShapeDtypeStruct((4, BS), F32),
        ),
        in_specs=[anywhere] * 7,
        out_specs=(vmem, vmem),
        scratch_shapes=[
            pltpu.VMEM((2, 11 * BS, 256), BF),
            pltpu.VMEM((3, LB * BS, 512), BF),
            pltpu.VMEM((4, 512, LB * BS), BF),
            pltpu.VMEM((LB, 8, BS, BS), BF),
            pltpu.SMEM((LB, 8), jnp.int32),
            pltpu.SMEM((LB, 8), jnp.int32),
            pltpu.VMEM((384, 128), F32),
            pltpu.VMEM((4, 1, 512), jnp.int32),
            pltpu.VMEM((4, 1, 512), F32),
            pltpu.VMEM((LB, BAND, BS, BS), BF),
            pltpu.VMEM((8, BS, BS), BF),
            pltpu.VMEM((8, BS, BS), BF),
            pltpu.VMEM((8, BS, BS), BF),
            pltpu.VMEM((8, BS, BS), BF),
            pltpu.VMEM((2, BS, BS), BF),
            pltpu.VMEM((2, BS, BS), BF),
            pltpu.VMEM((LB, BS, BAND * BS), BF),
            pltpu.VMEM((2, LB * BS, 256), BF),
            pltpu.VMEM((NZ, 16, 16, 256), BF),
            pltpu.VMEM((NY, 16, 16, 256), BF),
            ring_buffer, ring_buffer, ring_buffer, ring_buffer,
            pltpu.VMEM((16, 16, 256), BF),
            pltpu.VMEM((16, 16, 256), BF),
            pltpu.VMEM((16, 16, 256), BF),
            pltpu.VMEM((16, 16, 256), BF),
            pltpu.VMEM((NY, 4, BS), F32),
            pltpu.VMEM((16, 4, BS), F32),
            dma((8,)), dma((9,)), dma((9,)), dma((4,)), dma((4,)), dma((2, 8)), dma((2, 8)), dma((2,)),
            dma((2, 2)), dma((2, 2, 14)), dma((2,)), dma((2,)), dma((2,)), dma((2,)),
        ],
        compiler_params=pltpu.CompilerParams(
            collective_id=0, has_side_effects=True, vmem_limit_bytes=40 * 1024 * 1024
        ),
    )(
        *(
            pltpu.with_memory_space_constraint(array, pltpu.HBM)
            for array in (
                eigvec, operator_blocks, column_blocks, block_mask,
                spectrum.reshape(384, 128), mode_index.reshape(4, 1, 512),
                linewidth.reshape(4, 1, 512),
            )
        )
    )
    return tile.T, diff.reshape(512)


def solution(mesh):
    in_specs = (
        P("atoms", "modes"),
        P("atoms", None, None, None),
        P("atoms", None),
        P("atoms", None),
        P(),
        P(),
        P(),
    )
    out_specs = (P("modes", "atoms"), P("modes"))
    return jax.shard_map(body, mesh=mesh, in_specs=in_specs, out_specs=out_specs, check_vma=False)
```

```python
import functools

import jax
import jax.numpy as jnp
from jax import lax
from jax.experimental import pallas as pl
from jax.experimental.pallas import tpu as pltpu
from jax.sharding import PartitionSpec as P

BF = jnp.bfloat16
F32 = jnp.float32
NX, NZ, NY = 2, 8, 8
ATOMS = NX * NZ * NY
REACH = 4
BAND = 2 * REACH + 1
BS = 128
LB = 3
UP = ((0, 7), (0, 8), (1, 6), (1, 7), (1, 8), (2, 5), (2, 6), (2, 7), (2, 8))
DOWN = ((0, 1), (0, 2), (0, 3), (1, 0), (1, 1), (1, 2), (2, 0), (2, 1), (0, 0))


def kernel(
    e_hbm, op_hbm, col_hbm, mask_hbm, spec_hbm, midx_hbm, width_hbm,
    tile_ref, diff_ref,
    ext, others, turned, opv, col_s, mask_s, spec_ref, midx_ref, width_ref,
    dense, up_send, dn_send, lo_blk, hi_blk, far_out, far_in,
    bmat, wmat, pz, py, rz_plus, rz_minus, ry_plus, ry_minus, z_mid, y_mid, z_in, y_in,
    s_y, s_xz,
    load_sem, mode_send, mode_recv, blk_send, blk_recv, msg_send, msg_recv, past_send,
    ring_send, ring_recv, far_send, far_recv, sum_send, sum_recv,
):
    me = lax.axis_index("atoms")
    mode = lax.axis_index("modes")
    x_lo, core = mode // 2, mode % 2
    x, z, y = me // (NZ * NY), (me // NY) % NZ, me % NY
    above = ((me + 1) % ATOMS, mode)
    below = ((me + ATOMS - 1) % ATOMS, mode)
    twin = (me, x_lo * 2 + 1 - core)
    across = (me, (1 - x_lo) * 2 + core)
    twin_mode = x_lo * 2 + 1 - core
    across_mode = (1 - x_lo) * 2 + core
    last_mode = (1 - x_lo) * 2 + 1 - core

    def at_y(o):
        return (x * (NZ * NY) + z * NY + (y + o) % NY, mode)

    def at_z(o):
        return (x * (NZ * NY) + ((z + o) % NZ) * NY + y, mode)

    gz = x * NZ + z
    gy = x * NY + y

    def group_xz(o):
        g = (gz + o) % 16
        return g, (g * NY + y, mode)

    def group_xy(o):
        g = (gy + o) % 16
        return g, ((g // NY) * (NZ * NY) + z * NY + g % NY, mode)

    top = (y == NY - 1) & (z == NZ - 1)
    bottom = (y == 0) & (z == 0)
    before_top = (y == NY - 2) & (z == NZ - 1)
    before_bottom = (y == 1) & (z == 0)
    above_across = ((me + 1) % ATOMS, across_mode)
    below_across = ((me + ATOMS - 1) % ATOMS, across_mode)
    up_two_across = ((me + 2) % ATOMS, across_mode)
    down_two_across = ((me + ATOMS - 2) % ATOMS, across_mode)

    def remote(src, dst, ssem, rsem, device):
        return pltpu.make_async_remote_copy(
            src_ref=src, dst_ref=dst, send_sem=ssem, recv_sem=rsem,
            device_id=device, device_id_type=pl.DeviceIdType.MESH,
        )

    loads = (
        (op_hbm, opv), (col_hbm, col_s), (mask_hbm, mask_s),
        (e_hbm.at[:, pl.ds(0, 256)], ext.at[0, pl.ds(REACH * BS, LB * BS)]),
        (e_hbm.at[:, pl.ds(256, 256)], ext.at[1, pl.ds(REACH * BS, LB * BS)]),
        (spec_hbm, spec_ref), (midx_hbm, midx_ref), (width_hbm, width_ref),
    )
    loads = [pltpu.make_async_copy(a, b, load_sem.at[i]) for i, (a, b) in enumerate(loads)]
    for copy in loads:
        copy.start()

    barrier = pltpu.get_barrier_semaphore()

    def greet(device):
        pl.semaphore_signal(
            barrier, inc=1, device_id=device, device_id_type=pl.DeviceIdType.MESH
        )

    for device in (above, below, twin, across):
        greet(device)
    greet(((me + 2) % ATOMS, mode))
    greet(((me + ATOMS - 2) % ATOMS, mode))
    for o in range(1, 16):
        greet(group_xz(o)[1])
        greet(group_xy(o)[1])

    @pl.when(top)
    def _():
        greet(above_across)
        greet(up_two_across)

    @pl.when(bottom)
    def _():
        greet(below_across)
        greet(down_two_across)

    pl.when(before_top)(functools.partial(greet, up_two_across))
    pl.when(before_bottom)(functools.partial(greet, down_two_across))

    extra = jnp.where(top | bottom, 2, 0) + jnp.where(before_top | before_bottom, 1, 0)

    pl.semaphore_wait(barrier, 36 + extra)

    sends = []
    guarded = []

    def go(*args):
        copy = remote(*args)
        copy.start()
        sends.append(copy)
        return copy

    def arrived(dst, sem):
        remote(dst, dst, sem, sem, above).wait_recv()

    half = pl.ds(core * 4, 4)
    other_half = pl.ds((1 - core) * 4, 4)
    messages = [[(up_send.at[half], lo_blk.at[half])], [(dn_send.at[half], hi_blk.at[half])]]
    for h in range(2):
        lanes = pl.ds(h * 256, 256)
        rows = ext.at[h]
        messages[0] += [
            (e_hbm.at[pl.ds(256, 128), lanes], rows.at[pl.ds(384, 128)]),
            (e_hbm.at[pl.ds(0, 256), lanes], rows.at[pl.ds(128, 256)]),
            (rows.at[pl.ds(384, 128)], rows.at[pl.ds(0, 128)]),
        ]
        messages[1] += [
            (e_hbm.at[pl.ds(0, 128), lanes], rows.at[pl.ds(896, 128)]),
            (e_hbm.at[pl.ds(128, 256), lanes], rows.at[pl.ds(1024, 256)]),
            (rows.at[pl.ds(896, 128)], rows.at[pl.ds(1280, 128)]),
        ]
        if h == 0:
            messages[0].append(None)
            messages[1].append(None)

    def message(way, i):
        src, dst = messages[way][i]
        atoms, edge = (above[0], top) if way == 0 else (below[0], bottom)
        to_mode = jnp.where(edge, across_mode, mode) if i == 0 else mode
        return remote(src, dst, msg_send.at[way, i], msg_recv.at[way, i], (atoms, to_mode)), edge

    def tell(way, i):
        copy, edge = message(way, i)
        if i == 0:
            copy.start()
        else:
            pl.when(jnp.logical_not(edge))(copy.start)

    def past_corner(way, h):
        rows = pl.ds(2 * BS, BS) if way == 0 else pl.ds(0, BS)
        return remote(
            others.at[0, rows, pl.ds(h * 256, 256)], messages[way][4 * h + 3][1],
            past_send.at[h], msg_recv.at[way, 4 * h + 3], (up_two_across, down_two_across)[way],
        )

    def tell_past_corner(h):
        for way, edge in ((0, before_top), (1, before_bottom)):
            pl.when(edge)(past_corner(way, h).start)

    def tell_both(i):
        tell(0, i)
        tell(1, i)

    near_rows = pl.ds(pl.multiple_of(jnp.where(bottom | before_bottom, 0, 2 * BS), BS), BS)
    rest_rows = pl.ds(pl.multiple_of(jnp.where(bottom | before_bottom, BS, 0), BS), 2 * BS)
    pieces = (
        (near_rows, pl.ds(0, 256)), (near_rows, pl.ds(256, 256)),
        (rest_rows, pl.ds(0, 256)), (rest_rows, pl.ds(256, 256)),
    )

    def piece(n, p):
        return others.at[n, pieces[p][0], pieces[p][1]]

    def relay(p):
        for way, edge, device in ((0, top, above_across), (1, bottom, below_across)):

            @pl.when(edge)
            def _():
                i = (1, 5, 2, 6)[p]
                remote(
                    piece(0, p), messages[way][i][1],
                    msg_send.at[way, i], msg_recv.at[way, i], device,
                ).start()

    def hear(way, i):
        arrived(messages[way][i][1], msg_recv.at[way, i])

    for p in range(4):
        go(e_hbm.at[pieces[p][0], pieces[p][1]], piece(0, p), mode_send.at[p], mode_recv.at[p], across)
    go(e_hbm, others.at[1], mode_send.at[4], mode_recv.at[4], twin)
    tell_both(1)
    tell_both(5)

    for copy in loads[:3]:
        copy.wait()
    for r in range(LB):
        for d in range(BAND):
            target = (me * LB + r + d - REACH + ATOMS * LB) % (ATOMS * LB)
            slot = jnp.int32(0)
            used = jnp.int32(0)
            for s in range(8):
                hit = col_s[r, s] == target
                slot = jnp.where(hit, s, slot)
                used = jnp.where(hit, mask_s[r, s], used)
            keep = jnp.where(used > 0, F32(1), F32(0)).astype(F32)
            block = (opv[r, slot].astype(F32) * keep).astype(BF)
            dense[r, d] = block
            for n, (table, send) in enumerate(((UP, up_send), (DOWN, dn_send))):
                if (r, d) == table[8]:
                    far_out[n] = block
                elif (r, d) in table:
                    send[table.index((r, d))] = block

    tell_both(0)
    two_away = ((me + 2 - 4 * core + ATOMS) % ATOMS, mode)
    go(far_out.at[core], far_in.at[core], blk_send.at[2], blk_recv.at[2], two_away)
    tell_both(2)
    corner = top | bottom
    not_corner = jnp.logical_not(corner)
    pl.when(corner)(functools.partial(tell_both, 6))

    def build(r, d, mirror):
        value = mirror.astype(F32).T - dense[r, d].astype(F32)
        bmat[r, :, d * BS : (d + 1) * BS] = value.astype(BF)

    for copy in loads[3:]:
        copy.wait()
    for r in range(LB):
        for c in range(LB):
            d = c - r + REACH
            build(r, d, dense[c, 2 * REACH - d])
    for b in range(LB):
        for h in range(2):
            turned[mode, h * 256 : (h + 1) * 256, b * BS : (b + 1) * BS] = ext[
                h, (REACH + b) * BS : (REACH + b + 1) * BS
            ].T

    def turn_other(n, slot_mode, p):
        for b in range(LB):
            turned[slot_mode, p * BS : (p + 1) * BS, b * BS : (b + 1) * BS] = others[
                n, b * BS : (b + 1) * BS, p * BS : (p + 1) * BS
            ].T

    def hand_over(p):
        arrived(piece(0, p), mode_recv.at[p])
        relay(p)
        go(piece(0, p), piece(2, p), mode_send.at[5 + p], mode_recv.at[5 + p], twin)

    def pass_far(h):
        for way in (0, 1):
            hear(way, 4 * h + 1)
            tell(way, 4 * h + 3)

    def pass_both():
        pass_far(0)
        pass_far(1)

    for h in range(2):
        hand_over(h)
        tell_past_corner(h)

    @pl.when(not_corner)
    def _():
        pass_both()
        tell_both(6)

    hand_over(2)
    hear(0, 0)
    go(lo_blk.at[half], lo_blk.at[half], blk_send.at[0], blk_recv.at[0], twin)
    hear(1, 0)
    go(hi_blk.at[half], hi_blk.at[half], blk_send.at[1], blk_recv.at[1], twin)
    hand_over(3)
    pl.when(corner)(pass_both)
    arrived(far_in.at[core], blk_recv.at[2])
    go(far_in.at[core], far_in.at[core], blk_send.at[3], blk_recv.at[3], twin)
    for p in range(4):
        turn_other(0, across_mode, p)

    arrived(lo_blk.at[other_half], blk_recv.at[0])
    arrived(hi_blk.at[other_half], blk_recv.at[1])
    for k in range(8):
        c, d = UP[k]
        r = d + c - 7
        build(r, c + 1 - r, lo_blk[k])
        c, d = DOWN[k]
        r = d + c - 1
        build(r, c + 7 - r, hi_blk[k])

    arrived(others.at[1], mode_recv.at[4])
    for p in range(4):
        turn_other(1, twin_mode, p)
    for p in range(4):
        arrived(piece(2, p), mode_recv.at[5 + p])
    for p in range(4):
        turn_other(2, last_mode, p)

    arrived(far_in.at[1 - core], blk_recv.at[3])
    build(0, 0, far_in[0])
    build(2, 8, far_in[1])

    def apply_operator(h):
        for r in range(LB):
            wmat[h, r * BS : (r + 1) * BS, :] = jnp.dot(
                bmat[r], ext[h, r * BS : (r + BAND) * BS], preferred_element_type=F32
            ).astype(BF)

    def product(h):
        def step(mb, carry):
            part = jnp.dot(turned[mb], wmat[h], preferred_element_type=F32).astype(BF)
            for q in range(4):
                rows = part[q * BS : (q + 1) * BS].reshape(NY, 16, 256)
                if h == 0:
                    pz[(mb % 2) * 4 + q, pl.ds((mb // 2) * NY, NY)] = rows
                else:
                    py[:, mb * 4 + q] = rows
            return carry

        for mb in range(4):
            step(mb, 0)

    rings = (
        (pz, (rz_plus, rz_minus), z, at_z, 0),
        (py, (ry_plus, ry_minus), y, at_y, 1),
    )

    def owner(ring, sense, k):
        return (ring[2] + (k if sense == 0 else 8 - k)) % 8

    def hand(ring, sense, i, steps, src):
        device = ring[3](steps if sense == 0 else 8 - steps)
        r = ring[4]
        remote(
            src, ring[1][sense].at[i], ring_send.at[r, sense], ring_recv.at[r, sense, i], device
        ).start()

    def slot(h, k):
        return 2 + (3 - k) * 4 + h

    def quarters():
        for n in range(4):
            yield 0, (n + 2) % 4
            yield 1, n

    def begin(ring):
        for n, (sense, h) in enumerate(quarters()):
            src = ring[0].at[owner(ring, sense, 3), pl.ds(h * 4, 4)]
            hand(ring, sense, slot(h, 3), 1, src)
            if n != 3:
                continue
            for p in range(2):
                for way in range(2):
                    far = ring[0].at[owner(ring, way, 4), pl.ds((2 * way + p) * 4, 4)]
                    hand(ring, way, p, 2, far)

    def take(ring, sense, i):
        buf = ring[1][sense]
        arrived(buf.at[i], ring_recv.at[ring[4], sense, i])
        return buf[i]

    def advance(ring, k):
        for sense, h in quarters():
            i = slot(h, k)
            mine = ring[0][owner(ring, sense, k - 1), h * 4 : h * 4 + 4]
            buf = ring[1][sense]
            if k == 3 and h // 2 == sense:
                buf[i] = (
                    take(ring, sense, i).astype(F32) + mine.astype(F32)
                    + take(ring, sense, h % 2).astype(F32)
                ).astype(BF)
            else:
                buf[i] = take(ring, sense, i) + mine
            hand(ring, sense, slot(h, k - 1), 1, buf.at[i])

    def close(ring, mid, direct, own):
        for h in range(4):
            mine = ring[0][ring[2], h * 4 : h * 4 + 4].astype(F32)
            both = take(ring, 0, slot(h, 1)).astype(F32) + take(ring, 1, slot(h, 1)).astype(F32)
            mid[h * 4 : h * 4 + 4] = (mine + both).astype(BF)
            for g in range(h * 4, h * 4 + 4):
                pl.when(own != g)(direct((g - own + 16) % 16).start)

    def direct_z(o):
        g, device = group_xy(o)
        return remote(z_mid.at[g], z_in.at[gy], far_send.at[0], far_recv.at[0], device)

    def direct_y(o):
        g, device = group_xz(o)
        return remote(y_mid.at[g], y_in.at[gz], far_send.at[1], far_recv.at[1], device)

    def send_direct(direct):
        def step(o, carry):
            direct(o).start()
            return carry

        lax.fori_loop(1, 16, step, 0)

    hear(0, 2)
    hear(1, 2)
    hear(0, 3)
    hear(1, 3)
    apply_operator(0)
    product(0)
    begin(rings[0])
    hear(0, 6)
    hear(1, 6)
    hear(0, 7)
    hear(1, 7)
    apply_operator(1)
    product(1)
    begin(rings[1])
    advance(rings[0], 3)
    advance(rings[1], 3)
    advance(rings[0], 2)
    advance(rings[1], 2)
    close(rings[0], z_mid, direct_z, gy)
    close(rings[1], y_mid, direct_y, gz)
    z_in[gy] = z_mid[gy]
    y_in[gz] = y_mid[gz]

    spot = lax.broadcasted_iota(jnp.int32, (16, 512), 0) + (me % 32) * 16
    on_tile = lax.broadcasted_iota(jnp.int32, (16, 512), 1) == spot

    def column(row):
        spread = jnp.where(on_tile, jnp.broadcast_to(row, (16, 512)), F32(0))
        return jnp.sum(spread, axis=1, keepdims=True)

    def frequency(block):
        at = midx_ref[block]
        high = lax.broadcasted_iota(jnp.int32, (384, 512), 0) == jnp.broadcast_to(at // 128, (384, 512))
        rows = lax.dot_general(
            spec_ref[...], high.astype(F32), (((0,), (0,)), ((), ())),
            precision=lax.Precision.HIGHEST, preferred_element_type=F32,
        )
        low = lax.broadcasted_iota(jnp.int32, (128, 512), 0) == jnp.broadcast_to(at % 128, (128, 512))
        return jnp.sum(jnp.where(low, rows, F32(0)), axis=0, keepdims=True)

    row_freq = frequency(mode)
    row_width = width_ref[mode]
    col_freq = column(frequency(me // 32))
    col_width = column(width_ref[me // 32])
    freq_sum = row_freq + col_freq
    spacing = row_freq - col_freq
    mean_width = 0.5 * (row_width + col_width)
    factor = freq_sum * freq_sum / (4.0 * row_freq * col_freq)
    weight = factor * mean_width / (spacing * spacing + mean_width * mean_width)

    fifteen = pl.ds(0, 15)
    arrived(z_in.at[fifteen], far_recv.at[0])
    arrived(y_in.at[fifteen], far_recv.at[1])
    tile = jnp.concatenate(
        [jnp.sum(z_in[...].astype(F32), axis=0), jnp.sum(y_in[...].astype(F32), axis=0)], axis=1
    )
    tile_ref[...] = tile
    share = jnp.sum(weight * tile * tile, axis=0, keepdims=True)

    for q in range(4):
        s_y[y, q : q + 1, :] = share[:, q * BS : (q + 1) * BS]
    for o in range(1, NY):
        remote(s_y.at[y], s_y.at[y], sum_send.at[0], sum_recv.at[0], at_y(o)).start()
    arrived(s_y.at[pl.ds(0, 7)], sum_recv.at[0])
    s_xz[gz] = jnp.sum(s_y[...], axis=0)
    for o in range(1, 16):
        remote(
            s_xz.at[gz], s_xz.at[gz], sum_send.at[1], sum_recv.at[1], group_xz(o)[1]
        ).start()
    arrived(s_xz.at[fifteen], sum_recv.at[1])
    diff_ref[...] = jnp.sum(s_xz[...], axis=0) * F32(1.0 / 2048)

    for way in (0, 1):
        for i in (0, 1, 2, 3, 5, 6, 7):
            copy, edge = message(way, i)
            if i in (3, 7):
                guarded.append((edge, copy))
            else:
                sends.append(copy)
        for h in range(2):
            edge = (before_top, before_bottom)[way]
            guarded.append((jnp.logical_not(edge), past_corner(way, h)))
    for copy in sends:
        copy.wait_send()
    for skipped, copy in guarded:
        pl.when(jnp.logical_not(skipped))(copy.wait_send)

    for ref, sem in (
        (z_in.at[fifteen], far_send.at[0]), (y_in.at[fifteen], far_send.at[1]),
        (s_y.at[pl.ds(0, 7)], sum_send.at[0]), (s_xz.at[fifteen], sum_send.at[1]),
        (rz_plus, ring_send.at[0, 0]), (rz_minus, ring_send.at[0, 1]),
        (ry_plus, ring_send.at[1, 0]), (ry_minus, ring_send.at[1, 1]),
    ):
        remote(ref, ref, sem, sem, above).wait_send()


def body(eigvec, operator_blocks, column_blocks, block_mask, spectrum, mode_index, linewidth):
    anywhere = pl.BlockSpec(memory_space=pl.ANY)
    vmem = pl.BlockSpec(memory_space=pltpu.VMEM)
    dma = pltpu.SemaphoreType.DMA
    ring_buffer = pltpu.VMEM((14, 4, 16, 256), BF)
    tile, diff = pl.pallas_call(
        kernel,
        out_shape=(
            jax.ShapeDtypeStruct((16, 512), F32),
            jax.ShapeDtypeStruct((4, BS), F32),
        ),
        in_specs=[anywhere] * 7,
        out_specs=(vmem, vmem),
        scratch_shapes=[
            pltpu.VMEM((2, 11 * BS, 256), BF),
            pltpu.VMEM((3, LB * BS, 512), BF),
            pltpu.VMEM((4, 512, LB * BS), BF),
            pltpu.VMEM((LB, 8, BS, BS), BF),
            pltpu.SMEM((LB, 8), jnp.int32),
            pltpu.SMEM((LB, 8), jnp.int32),
            pltpu.VMEM((384, 128), F32),
            pltpu.VMEM((4, 1, 512), jnp.int32),
            pltpu.VMEM((4, 1, 512), F32),
            pltpu.VMEM((LB, BAND, BS, BS), BF),
            pltpu.VMEM((8, BS, BS), BF),
            pltpu.VMEM((8, BS, BS), BF),
            pltpu.VMEM((8, BS, BS), BF),
            pltpu.VMEM((8, BS, BS), BF),
            pltpu.VMEM((2, BS, BS), BF),
            pltpu.VMEM((2, BS, BS), BF),
            pltpu.VMEM((LB, BS, BAND * BS), BF),
            pltpu.VMEM((2, LB * BS, 256), BF),
            pltpu.VMEM((NZ, 16, 16, 256), BF),
            pltpu.VMEM((NY, 16, 16, 256), BF),
            ring_buffer, ring_buffer, ring_buffer, ring_buffer,
            pltpu.VMEM((16, 16, 256), BF),
            pltpu.VMEM((16, 16, 256), BF),
            pltpu.VMEM((16, 16, 256), BF),
            pltpu.VMEM((16, 16, 256), BF),
            pltpu.VMEM((NY, 4, BS), F32),
            pltpu.VMEM((16, 4, BS), F32),
            dma((8,)), dma((9,)), dma((9,)), dma((4,)), dma((4,)), dma((2, 8)), dma((2, 8)), dma((2,)),
            dma((2, 2)), dma((2, 2, 14)), dma((2,)), dma((2,)), dma((2,)), dma((2,)),
        ],
        compiler_params=pltpu.CompilerParams(
            collective_id=0, has_side_effects=True, vmem_limit_bytes=40 * 1024 * 1024
        ),
    )(
        *(
            pltpu.with_memory_space_constraint(array, pltpu.HBM)
            for array in (
                eigvec, operator_blocks, column_blocks, block_mask,
                spectrum.reshape(384, 128), mode_index.reshape(4, 1, 512),
                linewidth.reshape(4, 1, 512),
            )
        )
    )
    return tile.T, diff.reshape(512)


def solution(mesh):
    in_specs = (
        P("atoms", "modes"),
        P("atoms", None, None, None),
        P("atoms", None),
        P("atoms", None),
        P(),
        P(),
        P(),
    )
    out_specs = (P("modes", "atoms"), P("modes"))
    return jax.shard_map(body, mesh=mesh, in_specs=in_specs, out_specs=out_specs, check_vma=False)
```
